128 devices in a mesh: heads: 8 (over y, core), tokens: 8 (over x_hi, z), cols: 2 (over x_lo).
Axes of the slice: x: 4 (x_hi: 2, x_lo: 2; x = x_hi * 2 + x_lo), y: 4, z: 4, core: 2. Of those that a mesh axis runs over, the one named last changes fastest.
Arguments:
- query_in: bfloat16 [4096, 8192], P('tokens', ('heads', 'cols')), may hold values from -24 to 24
- key_in: bfloat16 [4096, 8192], P('tokens', ('heads', 'cols')), may hold values from -24 to 24
- value_in: bfloat16 [4096, 8192], P('tokens', ('heads', 'cols')), may hold values from -6 to 6
- out_grads: bfloat16 [4096, 8192], P('tokens', ('heads', 'cols')), may hold values from -6 to 6
- doc_starts: int32 [6], replicated, may hold values from 0 to 4095, as said below
Outputs:
- input_factor: float32 [8192, 8192], P('heads', ('tokens', 'cols'))
- grad_factor: float32 [8192, 8192], P('heads', ('tokens', 'cols'))
The draws below stay inside these ranges and needn't reach their ends.
Inputs may be any that keep to these rules, and one draw needn't show every extreme that they name: Strictly increasing with the first entry 0; document d runs from doc_starts[d] to the next start (the last one to 4096) - 1. One document holds (8 // 2 + 1) * 512 tokens.
All inputs are finite; a program needn't handle non-finite values.
Results may differ from the reference program's by a relative error of at most 0.0041.
Values may be sent and summed in bfloat16 or wider, within the bound.
No kernel may reach another device: no remote copies, remote signals or barrier semaphores. Data moves between devices by JAX's collectives and lax.ppermute only.
A program may use at most 128 MiB of HBM per device.

```python
import math
import jax
import jax.numpy as jnp
from jax import lax

HEAD_DIM = 128
TOK_DEV = 512
DOCS = 6
D = 8192
TOKENS = 4096


def cut_points(key):
    long_len = (TOKENS // TOK_DEV // 2 + 1) * TOK_DEV
    rest_len = TOKENS - long_len
    cut_picks = jax.random.permutation(jax.random.fold_in(key, 11), rest_len - 1)[:DOCS - 2] + 1
    bounds = jnp.concatenate([jnp.zeros((1,), jnp.int32), jnp.sort(cut_picks).astype(jnp.int32), jnp.full((1,), rest_len, jnp.int32)])
    others = bounds[1:] - bounds[:-1]
    long_slot = jax.random.randint(jax.random.fold_in(key, 13), (), 0, DOCS).astype(jnp.int32)
    slots = jnp.arange(DOCS, dtype=jnp.int32)
    other_index = jnp.clip(slots - (slots > long_slot).astype(jnp.int32), 0, DOCS - 2)
    doc_lengths = jnp.where(slots == long_slot, long_len, others[other_index]).astype(jnp.int32)
    return jnp.concatenate([jnp.zeros((1,), jnp.int32), jnp.cumsum(doc_lengths)[:-1].astype(jnp.int32)])


def draw_doc_starts(key, part):
    return cut_points(key)


def background(key, salt):
    return jnp.clip(jax.random.normal(jax.random.fold_in(key, salt), (TOKENS, D), jnp.float32), -4.0, 4.0)


def draw_key_in(key, part):
    result = background(key, 31)
    return result.astype(jnp.bfloat16)


def draw_query_in(key, part):
    result = background(key, 37)
    return result.astype(jnp.bfloat16)


def shard_levels(stream_key, extent, cuts, smallest, largest):
    def one(axis_at, blocks):
        draws = jax.random.uniform(jax.random.fold_in(jax.random.fold_in(stream_key, 6), axis_at), (blocks,), jnp.float32, smallest / len(cuts), largest / len(cuts))
        return jnp.repeat(jnp.exp(draws), extent[axis_at] // blocks).reshape((-1,) + (1,) * (len(extent) - axis_at - 1))

    loudness = one(*cuts[0])
    for cut in cuts[1:]:
        loudness = loudness * one(*cut)
    return loudness


def gaussian(own_key, shape, scale, limit, shards=(), kind=jnp.bfloat16):
    factor_of = shard_levels(own_key, shape, shards, -0.22, 0.18) if shards else 1.0
    values = jax.random.normal(own_key, shape, jnp.float32) * scale * factor_of
    return jnp.minimum(jnp.maximum(values, -limit), limit).astype(kind)


def setup_inputs(seed: int = 0) -> dict:
    seeds = jax.random.split(jax.random.key(seed), 6)
    return {
        "query_in": draw_query_in(jax.random.fold_in(seeds[5], 71), 0),
        "key_in": draw_key_in(jax.random.fold_in(seeds[5], 71), 0),
        "value_in": gaussian(seeds[2], (TOKENS, D), 1.0, 6.0, ((0, 8), (1, 16))),
        "out_grads": gaussian(seeds[3], (TOKENS, D), 1.0, 6.0, ((0, 8), (1, 16))),
        "doc_starts": draw_doc_starts(jax.random.fold_in(seeds[5], 71), 0),
    }


MASK_FLOOR = -1e+30

def document_ids(positions, doc_starts):
    return lax.optimization_barrier(jnp.sum((positions[:, None] >= doc_starts[None, :]).astype(jnp.int32), axis=1)) - 1

def reference(query_in, key_in, value_in, out_grads, doc_starts):
    all_tokens, row_width = query_in.shape
    head_count = row_width // HEAD_DIM
    positions = jnp.arange(all_tokens, dtype=jnp.int32)
    doc_ids = document_ids(positions, doc_starts)
    allowed = doc_ids[:, None] == doc_ids[None, :]
    score_scale = 1.0 / math.sqrt(HEAD_DIM)

    def per_head(head_index):
        col_begin = (head_index * HEAD_DIM).astype(jnp.int32)

        def select_cols(source):
            return lax.dynamic_slice_in_dim(source, col_begin, HEAD_DIM, 1).astype(jnp.float32)
        scores = jnp.dot(select_cols(query_in), select_cols(key_in).T, precision=lax.Precision.HIGHEST) * score_scale
        masked = jnp.where(allowed, scores, MASK_FLOOR)
        row_peak = lax.optimization_barrier(jnp.max(masked, axis=1))
        row_mass = lax.optimization_barrier(jnp.sum(jnp.where(allowed, jnp.exp(masked - row_peak[:, None]), 0.0), axis=1))
        log_total = row_peak + jnp.log(row_mass)
        weights = jnp.where(allowed, jnp.exp(scores - log_total[:, None]), 0.0).astype(jnp.bfloat16)
        weights = lax.optimization_barrier(weights).astype(jnp.float32)
        attended = jnp.dot(weights, select_cols(value_in), precision=lax.Precision.HIGHEST)
        grad_rows = jnp.dot(weights.T, select_cols(out_grads), precision=lax.Precision.HIGHEST)
        return (attended, grad_rows)
    attended, grad_rows = lax.map(per_head, jnp.arange(head_count, dtype=jnp.int32))
    attended = attended.transpose(1, 0, 2).reshape(all_tokens, row_width).astype(jnp.bfloat16)
    value_grads = grad_rows.transpose(1, 0, 2).reshape(all_tokens, row_width).astype(jnp.bfloat16)
    attended_wide = attended.astype(jnp.float32)
    grads_wide = value_grads.astype(jnp.float32)
    input_factor = jnp.dot(attended_wide.T, attended_wide, precision=lax.Precision.HIGHEST) / all_tokens
    grad_factor = jnp.dot(grads_wide.T, grads_wide, precision=lax.Precision.HIGHEST) / all_tokens
    return (input_factor, grad_factor)
```

```python
import math

import jax
import jax.numpy as jnp
from jax import lax
from jax.experimental import pallas as pl
from jax.experimental.pallas import tpu as pltpu
from jax.sharding import Mesh
from jax.sharding import PartitionSpec as P

HEAD_DIM = 128
X = ("xh", "xl")
MASK_FLOOR = -1e30
KEY_STEP = 512
QUERY_STEP = 256
VMEM_BYTES = 56 * 1024 * 1024


def attention_kernel(
    starts, where_ref, q_ref, g_ref, k_own, k_oth, v_own, v_oth,
    att_ref, near_ref, far_ref,
    k_all, v_all, v_turned, scores, grads, sems,
):
    half = q_ref.shape[0]
    half_id = where_ref[0]
    own_at = pl.multiple_of(half_id * half, half)
    oth_at = pl.multiple_of((1 - half_id) * half, half)
    copies = [
        pltpu.make_async_copy(k_own, k_all.at[pl.ds(own_at, half)], sems.at[0]),
        pltpu.make_async_copy(k_oth, k_all.at[pl.ds(oth_at, half)], sems.at[1]),
        pltpu.make_async_copy(v_own, v_all.at[pl.ds(own_at, half)], sems.at[2]),
        pltpu.make_async_copy(v_oth, v_all.at[pl.ds(oth_at, half)], sems.at[3]),
    ]
    for copy in copies:
        copy.start()
    grads[...] = jnp.zeros_like(grads)
    for copy in copies:
        copy.wait()
    all_tokens = 2 * half
    docs = starts.shape[0]
    for at in range(0, all_tokens, KEY_STEP):
        v_turned[:, at : at + KEY_STEP] = v_all[at : at + KEY_STEP, :].T
    scale = math.log2(math.e) / math.sqrt(HEAD_DIM)
    groups = KEY_STEP // 8

    def query_block(block, carry):
        row = pl.multiple_of(block * QUERY_STEP, QUERY_STEP)
        first = own_at + row
        last = first + QUERY_STEP - 1
        pos = first + lax.broadcasted_iota(jnp.int32, (1, QUERY_STEP), 1)
        begin = jnp.zeros((1, QUERY_STEP), jnp.int32)
        finish = jnp.full((1, QUERY_STEP), all_tokens, jnp.int32)
        lowest = jnp.int32(0)
        highest = jnp.int32(all_tokens)
        for d in range(docs):
            start = starts[d]
            lowest = jnp.where(start <= first, jnp.maximum(lowest, start), lowest)
            highest = jnp.where(start > last, jnp.minimum(highest, start), highest)
            begin = jnp.where(start <= pos, jnp.maximum(begin, start), begin)
            finish = jnp.where(start > pos, jnp.minimum(finish, start), finish)
        step_from = lowest // KEY_STEP
        step_to = (highest + KEY_STEP - 1) // KEY_STEP
        queries = q_ref[pl.ds(row, QUERY_STEP), :]
        cotangents = g_ref[pl.ds(row, QUERY_STEP), :]
        key_iota = lax.broadcasted_iota(jnp.int32, (KEY_STEP, QUERY_STEP), 0)

        def score_step(step, peak):
            at = pl.multiple_of(step * KEY_STEP, KEY_STEP)
            s = lax.dot_general(
                k_all[pl.ds(at, KEY_STEP), :], queries, (((1,), (1,)), ((), ())),
                preferred_element_type=jnp.float32,
            ) * scale
            allowed = (key_iota >= begin - at) & (key_iota < finish - at)
            s = jnp.where(allowed, s, MASK_FLOOR)
            scores[pl.ds(at, KEY_STEP), :] = s
            return jnp.maximum(peak, jnp.max(s.reshape(groups, 8, QUERY_STEP), axis=0))

        peak = lax.fori_loop(
            step_from, step_to, score_step, jnp.full((8, QUERY_STEP), MASK_FLOOR, jnp.float32)
        )
        peak = jnp.max(peak, axis=0, keepdims=True)

        def mass_step(step, mass):
            at = pl.multiple_of(step * KEY_STEP, KEY_STEP)
            e = jnp.exp2(scores[pl.ds(at, KEY_STEP), :] - peak)
            scores[pl.ds(at, KEY_STEP), :] = e
            return mass + jnp.sum(e.reshape(groups, 8, QUERY_STEP), axis=0)

        mass = lax.fori_loop(step_from, step_to, mass_step, jnp.zeros((8, QUERY_STEP), jnp.float32))
        share = 1.0 / jnp.sum(mass, axis=0, keepdims=True)

        def value_step(step, summed):
            at = pl.multiple_of(step * KEY_STEP, KEY_STEP)
            w = (scores[pl.ds(at, KEY_STEP), :] * share).astype(jnp.bfloat16)
            grads[pl.ds(at, KEY_STEP), :] += jnp.dot(
                w, cotangents, preferred_element_type=jnp.float32
            )
            return summed + jnp.dot(
                v_turned[:, pl.ds(at, KEY_STEP)], w, preferred_element_type=jnp.float32
            )

        summed = lax.fori_loop(
            step_from, step_to, value_step, jnp.zeros((HEAD_DIM, QUERY_STEP), jnp.float32)
        )
        att_ref[:, pl.ds(row, QUERY_STEP)] = summed.astype(jnp.bfloat16)
        return carry

    lax.fori_loop(0, half // QUERY_STEP, query_block, 0)
    for at in range(0, half, KEY_STEP):
        near_ref[:, at : at + KEY_STEP] = grads[pl.ds(own_at + at, KEY_STEP), :].T
        far_ref[:, at : at + KEY_STEP] = grads[pl.ds(oth_at + at, KEY_STEP), :].T


def attention(starts, half_id, q, g, k_own, k_oth, v_own, v_oth):
    half = q.shape[0]
    hbm = pl.BlockSpec(memory_space=pl.ANY)
    vmem = pl.BlockSpec(memory_space=pltpu.VMEM)
    smem = pl.BlockSpec(memory_space=pltpu.SMEM)
    return pl.pallas_call(
        attention_kernel,
        out_shape=(
            jax.ShapeDtypeStruct((HEAD_DIM, half), jnp.bfloat16),
            jax.ShapeDtypeStruct((HEAD_DIM, half), jnp.float32),
            jax.ShapeDtypeStruct((HEAD_DIM, half), jnp.float32),
        ),
        in_specs=[smem, smem, vmem, vmem, hbm, hbm, hbm, hbm],
        out_specs=(vmem, vmem, vmem),
        scratch_shapes=[
            pltpu.VMEM((2 * half, HEAD_DIM), jnp.bfloat16),
            pltpu.VMEM((2 * half, HEAD_DIM), jnp.bfloat16),
            pltpu.VMEM((HEAD_DIM, 2 * half), jnp.bfloat16),
            pltpu.VMEM((2 * half, QUERY_STEP), jnp.float32),
            pltpu.VMEM((2 * half, HEAD_DIM), jnp.float32),
            pltpu.SemaphoreType.DMA((4,)),
        ],
        compiler_params=pltpu.CompilerParams(vmem_limit_bytes=VMEM_BYTES),
        name="attention",
    )(starts, half_id, q, g, k_own, k_oth, v_own, v_oth)


def shifted(x, axis, by):
    count = lax.axis_size(axis)
    return lax.ppermute(x, axis, [(i, (i + by) % count) for i in range(count)])


def ring(x, axis):
    half = x.shape[0] // 2
    below, above = shifted(x, axis, 1), shifted(x, axis, -1)
    far = (shifted(below[:half], axis, 1), shifted(above[half:], axis, -1))
    return (x, below, above, *far)


def stack_kernel(*refs):
    count = len(refs) - 2
    parts, out, sems = refs[:count], refs[count], refs[count + 1]
    copies, at = [], 0
    for k, part in enumerate(parts):
        rows = part.shape[0]
        copies.append(pltpu.make_async_copy(part, out.at[pl.ds(at, rows)], sems.at[k]))
        at += rows
    for copy in copies:
        copy.start()
    for copy in copies:
        copy.wait()


def stacked(parts):
    rows = sum(p.shape[0] for p in parts)
    hbm = pl.BlockSpec(memory_space=pl.ANY)
    return pl.pallas_call(
        stack_kernel,
        out_shape=jax.ShapeDtypeStruct((rows, *parts[0].shape[1:]), parts[0].dtype),
        in_specs=[hbm] * len(parts),
        out_specs=hbm,
        scratch_shapes=[pltpu.SemaphoreType.DMA((len(parts),))],
        name="stack",
    )(*parts)


def factor_kernel(place, *refs, z_first, count):
    row_refs, own_cols, oth_cols = refs[:5], refs[5:10], refs[10:15]
    out, rows, cols, sems = refs[15], refs[16], refs[17], refs[18]
    x, y, z, core = place[0], place[1], place[2], place[3]
    block = HEAD_DIM
    half = block // 2
    copies = []

    def start(src, dst):
        copy = pltpu.make_async_copy(src, dst, sems.at[len(copies)])
        copy.start()
        copies.append(copy)

    ring_steps = (0, 3, 1, 2)
    for who, parts in ((core, own_cols), (1 - core, oth_cols)):
        for k in range(5):
            if k < 3:
                at = pl.multiple_of(((y + ring_steps[k]) % 4) * block, block)
                start(parts[k], cols.at[who, pl.ds(at, block)])
            else:
                at = pl.multiple_of(((y + 2) % 4) * block + (k - 3) * half, half)
                start(parts[k], cols.at[who, pl.ds(at, half)])
    for k in range(5):
        outer = ring_steps[min(k, 3)]
        inners = ((0, 1, 2, 3), (0, 1, 2, 3), (0, 1, 2, 3), (0, 1), (2, 3))[k]
        for n, slot in enumerate(inners):
            inner = ring_steps[slot]
            zz = (z + (inner if z_first else outer)) % 4
            xx = (x + (outer if z_first else inner)) % 4
            at = pl.multiple_of(((xx % 2) * 4 + zz) * block, block)
            start(row_refs[k].at[pl.ds(n * block, block)], rows.at[xx // 2, pl.ds(at, block)])
    for copy in copies:
        copy.wait()
    step = 256
    for at in range(0, rows.shape[1], step):
        total = None
        for who in range(2):
            part = lax.dot_general(
                rows[who, at : at + step, :], cols[who], (((1,), (1,)), ((), ())),
                preferred_element_type=jnp.float32,
            )
            total = part if total is None else total + part
        out[at : at + step, :] = total * (1.0 / count)


def factor(place, rows, own_cols, oth_cols, z_first, count):
    tokens = own_cols[0].shape[1]
    hbm = pl.BlockSpec(memory_space=pl.ANY)
    kernel = lambda *refs: factor_kernel(*refs, z_first=z_first, count=count)
    return pl.pallas_call(
        kernel,
        out_shape=jax.ShapeDtypeStruct((8 * HEAD_DIM, 4 * HEAD_DIM), jnp.float32),
        in_specs=[pl.BlockSpec(memory_space=pltpu.SMEM)] + [hbm] * 15,
        out_specs=pl.BlockSpec(memory_space=pltpu.VMEM),
        scratch_shapes=[
            pltpu.VMEM((2, 8 * HEAD_DIM, tokens), jnp.bfloat16),
            pltpu.VMEM((2, 4 * HEAD_DIM, tokens), jnp.bfloat16),
            pltpu.SemaphoreType.DMA((26,)),
        ],
        compiler_params=pltpu.CompilerParams(vmem_limit_bytes=VMEM_BYTES),
        name="factor_z_first" if z_first else "factor_x_first",
    )(place, *rows, *own_cols, *oth_cols)


def by_head(x):
    return lax.all_to_all(x, "z", split_axis=1, concat_axis=0, tiled=True)


def column_moves():
    def index(y, core, xh, z):
        return ((y * 2 + core) * 2 + xh) * 4 + z

    moves = []
    for y in range(4):
        for core in range(2):
            for xh in range(2):
                for z in range(4):
                    heads = y * 2 + core
                    moves.append((index(y, core, xh, z), index(z, xh, heads // 4, heads % 4)))
    return moves


def on_device(query_in, key_in, value_in, out_grads, doc_starts):
    all_tokens = query_in.shape[0] * 8
    xh, z = lax.axis_index("xh"), lax.axis_index("z")
    place = jnp.stack(
        [lax.axis_index(X), lax.axis_index("y"), z, lax.axis_index("core")]
    ).astype(jnp.int32)
    k_own = by_head(key_in)
    k_oth = shifted(k_own, "xh", 1)
    v_own = by_head(value_in)
    v_oth = shifted(v_own, "xh", 1)
    q, g = by_head(query_in), by_head(out_grads)
    attended, near, far = attention(
        doc_starts, xh.astype(jnp.int32)[None], q, g, k_own, k_oth, v_own, v_oth
    )
    value_grads = (near + shifted(far, "xh", 1)).astype(jnp.bfloat16)

    def columns(tile):
        moved = lax.ppermute(tile, ("y", "core", "xh", "z"), column_moves())
        own = ring(moved, "y")
        other = tuple(shifted(p, "core", 1) for p in own)
        return own, other

    own_a, oth_a = columns(attended)
    rows_a = ring(stacked(ring(attended, X)), "z")
    own_g, oth_g = columns(value_grads)
    rows_g = ring(stacked(ring(value_grads, "z")), X)
    input_factor = factor(place, rows_a, own_a, oth_a, False, all_tokens)
    grad_factor = factor(place, rows_g, own_g, oth_g, True, all_tokens)
    return (input_factor, grad_factor)


def solution(mesh):
    split = Mesh(mesh.devices.reshape(4, 2, 2, 4, 2), ("y", "core", "xh", "z", "xl"))
    tokens, features = ("xh", "z"), ("y", "core", "xl")
    spec = P(tokens, features)
    out = P(("y", "core"), ("xh", "z", "xl"))
    return jax.shard_map(
        on_device, mesh=split, in_specs=(spec, spec, spec, spec, P()), out_specs=(out, out),
        check_vma=False,
    )
```

```python
import functools
import math

import jax
import jax.numpy as jnp
from jax import lax
from jax.experimental import pallas as pl
from jax.experimental.pallas import tpu as pltpu
from jax.sharding import Mesh
from jax.sharding import PartitionSpec as P

HEAD_DIM = 128
X = ("xh", "xl")
MASK_FLOOR = -1e30
KEY_STEP = 512
QUERY_STEP = 512
VMEM_BYTES = 56 * 1024 * 1024


def attention_kernel(
    starts, where_ref, q_ref, g_ref, k_own, k_oth, v_own, v_oth,
    att_ref, near_ref, far_ref,
    k_all, v_all, v_turned, scores, grads, sems,
):
    half = q_ref.shape[0]
    half_id = where_ref[0]
    own_at = pl.multiple_of(half_id * half, half)
    oth_at = pl.multiple_of((1 - half_id) * half, half)
    copies = [
        pltpu.make_async_copy(k_own, k_all.at[pl.ds(own_at, half)], sems.at[0]),
        pltpu.make_async_copy(k_oth, k_all.at[pl.ds(oth_at, half)], sems.at[1]),
        pltpu.make_async_copy(v_own, v_all.at[pl.ds(own_at, half)], sems.at[2]),
        pltpu.make_async_copy(v_oth, v_all.at[pl.ds(oth_at, half)], sems.at[3]),
    ]
    for copy in copies:
        copy.start()
    grads[...] = jnp.zeros_like(grads)
    for copy in copies:
        copy.wait()
    all_tokens = 2 * half
    docs = starts.shape[0]
    for at in range(0, all_tokens, KEY_STEP):
        v_turned[:, at : at + KEY_STEP] = v_all[at : at + KEY_STEP, :].T
    scale = math.log2(math.e) / math.sqrt(HEAD_DIM)
    groups = KEY_STEP // 8

    def query_block(block, carry):
        row = pl.multiple_of(block * QUERY_STEP, QUERY_STEP)
        first = own_at + row
        last = first + QUERY_STEP - 1
        pos = first + lax.broadcasted_iota(jnp.int32, (1, QUERY_STEP), 1)
        begin = jnp.zeros((1, QUERY_STEP), jnp.int32)
        finish = jnp.full((1, QUERY_STEP), all_tokens, jnp.int32)
        lowest, latest = jnp.int32(0), jnp.int32(0)
        highest, soonest = jnp.int32(all_tokens), jnp.int32(all_tokens)
        for d in range(docs):
            start = starts[d]
            lowest = jnp.where(start <= first, jnp.maximum(lowest, start), lowest)
            highest = jnp.where(start > last, jnp.minimum(highest, start), highest)
            latest = jnp.where(start <= last, jnp.maximum(latest, start), latest)
            soonest = jnp.where(start > first, jnp.minimum(soonest, start), soonest)
            begin = jnp.where(start <= pos, jnp.maximum(begin, start), begin)
            finish = jnp.where(start > pos, jnp.minimum(finish, start), finish)
        step_from = lowest // KEY_STEP
        step_to = (highest + KEY_STEP - 1) // KEY_STEP
        inside_from = jnp.minimum((latest + KEY_STEP - 1) // KEY_STEP, step_to)
        inside_to = jnp.maximum(soonest // KEY_STEP, inside_from)
        queries = q_ref[pl.ds(row, QUERY_STEP), :]
        cotangents = g_ref[pl.ds(row, QUERY_STEP), :]
        key_iota = lax.broadcasted_iota(jnp.int32, (KEY_STEP, QUERY_STEP), 0)

        def score_step(step, peak, masked):
            at = pl.multiple_of(step * KEY_STEP, KEY_STEP)
            s = lax.dot_general(
                k_all[pl.ds(at, KEY_STEP), :], queries, (((1,), (1,)), ((), ())),
                preferred_element_type=jnp.float32,
            ) * scale
            if masked:
                allowed = (key_iota >= begin - at) & (key_iota < finish - at)
                s = jnp.where(allowed, s, MASK_FLOOR)
            scores[pl.ds(at, KEY_STEP), :] = s
            return jnp.maximum(peak, jnp.max(s.reshape(groups, 8, QUERY_STEP), axis=0))

        edge_step = functools.partial(score_step, masked=True)
        inside_step = functools.partial(score_step, masked=False)
        peak = jnp.full((8, QUERY_STEP), MASK_FLOOR, jnp.float32)
        peak = lax.fori_loop(step_from, inside_from, edge_step, peak)
        peak = lax.fori_loop(inside_from, inside_to, inside_step, peak)
        peak = lax.fori_loop(inside_to, step_to, edge_step, peak)
        peak = jnp.max(peak, axis=0, keepdims=True)

        def mass_step(step, mass):
            at = pl.multiple_of(step * KEY_STEP, KEY_STEP)
            e = jnp.exp2(scores[pl.ds(at, KEY_STEP), :] - peak)
            scores[pl.ds(at, KEY_STEP), :] = e
            return mass + jnp.sum(e.reshape(groups, 8, QUERY_STEP), axis=0)

        mass = lax.fori_loop(step_from, step_to, mass_step, jnp.zeros((8, QUERY_STEP), jnp.float32))
        share = 1.0 / jnp.sum(mass, axis=0, keepdims=True)

        def value_step(step, summed):
            at = pl.multiple_of(step * KEY_STEP, KEY_STEP)
            w = (scores[pl.ds(at, KEY_STEP), :] * share).astype(jnp.bfloat16)
            grads[pl.ds(at, KEY_STEP), :] += jnp.dot(
                w, cotangents, preferred_element_type=jnp.float32
            )
            return summed + jnp.dot(
                v_turned[:, pl.ds(at, KEY_STEP)], w, preferred_element_type=jnp.float32
            )

        summed = lax.fori_loop(
            step_from, step_to, value_step, jnp.zeros((HEAD_DIM, QUERY_STEP), jnp.float32)
        )
        att_ref[:, pl.ds(row, QUERY_STEP)] = summed.astype(jnp.bfloat16)
        return carry

    lax.fori_loop(0, half // QUERY_STEP, query_block, 0)
    for at in range(0, half, KEY_STEP):
        near_ref[:, at : at + KEY_STEP] = grads[pl.ds(own_at + at, KEY_STEP), :].T
        far_ref[:, at : at + KEY_STEP] = grads[pl.ds(oth_at + at, KEY_STEP), :].T.astype(jnp.bfloat16)


def attention(starts, half_id, q, g, k_own, k_oth, v_own, v_oth):
    half = q.shape[0]
    hbm = pl.BlockSpec(memory_space=pl.ANY)
    vmem = pl.BlockSpec(memory_space=pltpu.VMEM)
    smem = pl.BlockSpec(memory_space=pltpu.SMEM)
    return pl.pallas_call(
        attention_kernel,
        out_shape=(
            jax.ShapeDtypeStruct((HEAD_DIM, half), jnp.bfloat16),
            jax.ShapeDtypeStruct((HEAD_DIM, half), jnp.float32),
            jax.ShapeDtypeStruct((HEAD_DIM, half), jnp.bfloat16),
        ),
        in_specs=[smem, smem, vmem, vmem, hbm, hbm, hbm, hbm],
        out_specs=(vmem, vmem, vmem),
        scratch_shapes=[
            pltpu.VMEM((2 * half, HEAD_DIM), jnp.bfloat16),
            pltpu.VMEM((2 * half, HEAD_DIM), jnp.bfloat16),
            pltpu.VMEM((HEAD_DIM, 2 * half), jnp.bfloat16),
            pltpu.VMEM((2 * half, QUERY_STEP), jnp.float32),
            pltpu.VMEM((2 * half, HEAD_DIM), jnp.float32),
            pltpu.SemaphoreType.DMA((4,)),
        ],
        compiler_params=pltpu.CompilerParams(vmem_limit_bytes=VMEM_BYTES),
        name="attention",
    )(starts, half_id, q, g, k_own, k_oth, v_own, v_oth)


def shifted(x, axis, by):
    count = lax.axis_size(axis)
    return lax.ppermute(x, axis, [(i, (i + by) % count) for i in range(count)])


def near_ring(x, axis):
    return shifted(x, axis, 1), shifted(x, axis, -1)


def far_ring(below, above, axis):
    half = below.shape[0] // 2
    return shifted(below[:half], axis, 1), shifted(above[half:], axis, -1)


def ring(x, axis):
    below, above = near_ring(x, axis)
    return (x, below, above, *far_ring(below, above, axis))


def stack_kernel(*refs):
    out, at = refs[-1], 0
    for part in refs[:-1]:
        out[at : at + part.shape[0], :] = part[...]
        at += part.shape[0]


def stacked(parts):
    rows = sum(p.shape[0] for p in parts)
    vmem = pl.BlockSpec(memory_space=pltpu.VMEM)
    return pl.pallas_call(
        stack_kernel,
        out_shape=jax.ShapeDtypeStruct((rows, *parts[0].shape[1:]), parts[0].dtype),
        in_specs=[vmem] * len(parts),
        out_specs=vmem,
        name="stack",
    )(*parts)


def factor_kernel(place, *refs, which, count):
    z_first = which == 0
    row_refs, (col_ref, out, rows, cols, sems) = refs[:5], refs[5:]
    x, z = place[0], place[1]
    block = HEAD_DIM
    copies = []

    def start(src, dst):
        copy = pltpu.make_async_copy(src, dst, sems.at[len(copies)])
        copy.start()
        copies.append(copy)

    ring_steps = (0, 3, 1, 2)
    line = 4 - (x // 2) * 2 - z // 2
    for n in range(8):
        at = ((n // 2 + line) % 4) * block
        start(col_ref.at[pl.ds(n * block, block)], cols.at[n % 2, pl.ds(pl.multiple_of(at, block), block)])
    for k in range(5):
        outer = ring_steps[min(k, 3)]
        inners = ((0, 1, 2, 3), (0, 1, 2, 3), (0, 1, 2, 3), (0, 1), (2, 3))[k]
        for n, slot in enumerate(inners):
            inner = ring_steps[slot]
            zz = (z + (inner if z_first else outer)) % 4
            xx = (x + (outer if z_first else inner)) % 4
            at = pl.multiple_of(((xx % 2) * 4 + zz) * block, block)
            start(row_refs[k].at[pl.ds(n * block, block)], rows.at[xx // 2, pl.ds(at, block)])
    for copy in copies:
        copy.wait()
    step = 256
    for at in range(0, rows.shape[1], step):
        total = None
        for who in range(2):
            part = lax.dot_general(
                rows[who, at : at + step, :], cols[who], (((1,), (1,)), ((), ())),
                preferred_element_type=jnp.float32,
            )
            total = part if total is None else total + part
        out[at : at + step, :] = total * (1.0 / count)


def factor(place, rows, cols, which, count):
    tokens = cols.shape[1]
    hbm = pl.BlockSpec(memory_space=pl.ANY)
    kernel = lambda *refs: factor_kernel(*refs, which=which, count=count)
    return pl.pallas_call(
        kernel,
        out_shape=jax.ShapeDtypeStruct((8 * HEAD_DIM, 4 * HEAD_DIM), jnp.float32),
        in_specs=[pl.BlockSpec(memory_space=pltpu.SMEM)] + [hbm] * 6,
        out_specs=pl.BlockSpec(memory_space=pltpu.VMEM),
        scratch_shapes=[
            pltpu.VMEM((2, 8 * HEAD_DIM, tokens), jnp.bfloat16),
            pltpu.VMEM((2, 4 * HEAD_DIM, tokens), jnp.bfloat16),
            pltpu.SemaphoreType.DMA((24,)),
        ],
        compiler_params=pltpu.CompilerParams(vmem_limit_bytes=VMEM_BYTES),
        name="grad_factor" if which else "input_factor",
    )(place, *rows, cols)


def by_head(x):
    return lax.all_to_all(x, "z", split_axis=1, concat_axis=0, tiled=True)


def column_moves():
    ranks = [(y, core, xh, z) for y in range(4) for core in range(2) for xh in range(2) for z in range(4)]
    place = {rank: n for n, rank in enumerate(ranks)}
    along_y, in_plane = [], []
    for y, core, xh, z in ranks:
        spread = (y + z) % 4
        along_y.append((place[y, core, xh, z], place[spread, core, xh, z]))
        in_plane.append((place[spread, core, xh, z], place[spread, xh, y // 2, (y % 2) * 2 + core]))
    return along_y, in_plane


def on_device(query_in, key_in, value_in, out_grads, doc_starts):
    all_tokens = query_in.shape[0] * 8
    xh, z = lax.axis_index("xh"), lax.axis_index("z")
    place = jnp.stack([lax.axis_index(X), z]).astype(jnp.int32)
    k_own = by_head(key_in)
    k_oth = shifted(k_own, "xh", 1)
    v_own = by_head(value_in)
    v_oth = shifted(v_own, "xh", 1)
    q, g = by_head(query_in), by_head(out_grads)
    attended, near, far = attention(
        doc_starts, xh.astype(jnp.int32)[None], q, g, k_own, k_oth, v_own, v_oth
    )
    line = ("y", "core", "xh", "z")
    along_y, in_plane = column_moves()
    far = shifted(far, "xh", 1)
    a_near = near_ring(attended, "z")
    a_col = lax.ppermute(attended, line, along_y)
    near, far, attended, a_near, a_col = lax.optimization_barrier((near, far, attended, a_near, a_col))
    value_grads = (near + far).astype(jnp.bfloat16)
    g_near = near_ring(value_grads, X)
    g_col = lax.ppermute(value_grads, line, along_y)
    a_far = far_ring(*a_near, "z")
    a_col = lax.ppermute(a_col, line, in_plane)
    a_near, a_far, a_col, value_grads, g_near, g_col = lax.optimization_barrier(
        (a_near, a_far, a_col, value_grads, g_near, g_col)
    )
    group_a = stacked((attended, *a_near, *a_far))
    g_far = far_ring(*g_near, X)
    g_col = lax.ppermute(g_col, line, in_plane)
    group_g = stacked((value_grads, *g_near, *g_far))
    cols_a = lax.all_gather(a_col, ("y", "core"), axis=0, tiled=True)
    cols_g = lax.all_gather(g_col, ("y", "core"), axis=0, tiled=True)
    rows_a = ring(group_a, X)
    rows_g = ring(group_g, "z")
    input_factor = factor(place, rows_a, cols_a, 0, all_tokens)
    grad_factor = factor(place, rows_g, cols_g, 1, all_tokens)
    return (input_factor, grad_factor)


def solution(mesh):
    split = Mesh(mesh.devices.reshape(4, 2, 2, 4, 2), ("y", "core", "xh", "z", "xl"))
    tokens, features = ("xh", "z"), ("y", "core", "xl")
    spec = P(tokens, features)
    out = P(("y", "core"), ("xh", "z", "xl"))
    return jax.shard_map(
        on_device, mesh=split, in_specs=(spec, spec, spec, spec, P()), out_specs=(out, out),
        check_vma=False,
    )
```

```python
import functools
import math

import jax
import jax.numpy as jnp
from jax import lax
from jax.experimental import pallas as pl
from jax.experimental.pallas import tpu as pltpu
from jax.sharding import Mesh
from jax.sharding import PartitionSpec as P

HEAD_DIM = 128
X = ("xh", "xl")
RING = (0, 3, 1, 2)
MASK_FLOOR = -1e30
KEY_STEP = 512
QUERY_STEP = 512
VMEM_BYTES = 56 * 1024 * 1024


def attention_kernel(starts, where_ref, *refs):
    kv_own, kv_oth, qg = refs[:4], refs[4:8], refs[8:12]
    att_ref, near_ref, far_ref = refs[12:15]
    k_all, v_all, q_ref, g_ref, v_turned, scores, grads, sems = refs[15:]
    half = q_ref.shape[0]
    part = half // 4
    half_id, z = where_ref[0], where_ref[1]
    own_at = pl.multiple_of(half_id * half, half)
    oth_at = pl.multiple_of((1 - half_id) * half, half)
    copies = []
    for pieces, base, targets in (
        (kv_own, own_at, (k_all, v_all)), (kv_oth, oth_at, (k_all, v_all)), (qg, 0, (q_ref, g_ref))
    ):
        for step, piece in zip(RING, pieces):
            at = pl.multiple_of(base + ((z + step) % 4) * part, part)
            for n, target in enumerate(targets):
                copies.append(
                    pltpu.make_async_copy(
                        piece.at[pl.ds(n * part, part)], target.at[pl.ds(at, part)], sems.at[len(copies)]
                    )
                )
    for copy in copies:
        copy.start()
    grads[...] = jnp.zeros_like(grads)
    for copy in copies:
        copy.wait()
    all_tokens = 2 * half
    docs = starts.shape[0]
    for at in range(0, all_tokens, KEY_STEP):
        v_turned[:, at : at + KEY_STEP] = v_all[at : at + KEY_STEP, :].T
    scale = math.log2(math.e) / math.sqrt(HEAD_DIM)
    groups = KEY_STEP // 8

    def query_block(block, carry):
        row = pl.multiple_of(block * QUERY_STEP, QUERY_STEP)
        first = own_at + row
        last = first + QUERY_STEP - 1
        pos = first + lax.broadcasted_iota(jnp.int32, (1, QUERY_STEP), 1)
        begin = jnp.zeros((1, QUERY_STEP), jnp.int32)
        finish = jnp.full((1, QUERY_STEP), all_tokens, jnp.int32)
        lowest, latest = jnp.int32(0), jnp.int32(0)
        highest, soonest = jnp.int32(all_tokens), jnp.int32(all_tokens)
        for d in range(docs):
            start = starts[d]
            lowest = jnp.where(start <= first, jnp.maximum(lowest, start), lowest)
            highest = jnp.where(start > last, jnp.minimum(highest, start), highest)
            latest = jnp.where(start <= last, jnp.maximum(latest, start), latest)
            soonest = jnp.where(start > first, jnp.minimum(soonest, start), soonest)
            begin = jnp.where(start <= pos, jnp.maximum(begin, start), begin)
            finish = jnp.where(start > pos, jnp.minimum(finish, start), finish)
        step_from = lowest // KEY_STEP
        step_to = (highest + KEY_STEP - 1) // KEY_STEP
        inside_from = jnp.minimum((latest + KEY_STEP - 1) // KEY_STEP, step_to)
        inside_to = jnp.maximum(soonest // KEY_STEP, inside_from)
        queries = q_ref[pl.ds(row, QUERY_STEP), :]
        cotangents = g_ref[pl.ds(row, QUERY_STEP), :]
        key_iota = lax.broadcasted_iota(jnp.int32, (KEY_STEP, QUERY_STEP), 0)

        def score_step(step, peak, masked):
            at = pl.multiple_of(step * KEY_STEP, KEY_STEP)
            s = lax.dot_general(
                k_all[pl.ds(at, KEY_STEP), :], queries, (((1,), (1,)), ((), ())),
                preferred_element_type=jnp.float32,
            ) * scale
            if masked:
                allowed = (key_iota >= begin - at) & (key_iota < finish - at)
                s = jnp.where(allowed, s, MASK_FLOOR)
            scores[pl.ds(at, KEY_STEP), :] = s
            return jnp.maximum(peak, jnp.max(s.reshape(groups, 8, QUERY_STEP), axis=0))

        edge_step = functools.partial(score_step, masked=True)
        inside_step = functools.partial(score_step, masked=False)
        peak = jnp.full((8, QUERY_STEP), MASK_FLOOR, jnp.float32)
        peak = lax.fori_loop(step_from, inside_from, edge_step, peak)
        peak = lax.fori_loop(inside_from, inside_to, inside_step, peak)
        peak = lax.fori_loop(inside_to, step_to, edge_step, peak)
        peak = jnp.max(peak, axis=0, keepdims=True)

        def mass_step(step, mass):
            at = pl.multiple_of(step * KEY_STEP, KEY_STEP)
            e = jnp.exp2(scores[pl.ds(at, KEY_STEP), :] - peak)
            scores[pl.ds(at, KEY_STEP), :] = e
            return mass + jnp.sum(e.reshape(groups, 8, QUERY_STEP), axis=0)

        mass = lax.fori_loop(step_from, step_to, mass_step, jnp.zeros((8, QUERY_STEP), jnp.float32))
        share = 1.0 / jnp.sum(mass, axis=0, keepdims=True)

        def value_step(step, summed):
            at = pl.multiple_of(step * KEY_STEP, KEY_STEP)
            w = (scores[pl.ds(at, KEY_STEP), :] * share).astype(jnp.bfloat16)
            grads[pl.ds(at, KEY_STEP), :] += jnp.dot(
                w, cotangents, preferred_element_type=jnp.float32
            )
            return summed + jnp.dot(
                v_turned[:, pl.ds(at, KEY_STEP)], w, preferred_element_type=jnp.float32
            )

        summed = lax.fori_loop(
            step_from, step_to, value_step, jnp.zeros((HEAD_DIM, QUERY_STEP), jnp.float32)
        )
        att_ref[:, pl.ds(row, QUERY_STEP)] = summed.astype(jnp.bfloat16)
        return carry

    lax.fori_loop(0, half // QUERY_STEP, query_block, 0)
    for at in range(0, half, KEY_STEP):
        near_ref[:, at : at + KEY_STEP] = grads[pl.ds(own_at + at, KEY_STEP), :].T
        far_ref[:, at : at + KEY_STEP] = grads[pl.ds(oth_at + at, KEY_STEP), :].T.astype(jnp.bfloat16)


def attention(starts, where, kv_own, kv_oth, qg):
    half = 2 * qg[0].shape[0]
    hbm = pl.BlockSpec(memory_space=pl.ANY)
    vmem = pl.BlockSpec(memory_space=pltpu.VMEM)
    smem = pl.BlockSpec(memory_space=pltpu.SMEM)
    return pl.pallas_call(
        attention_kernel,
        out_shape=(
            jax.ShapeDtypeStruct((HEAD_DIM, half), jnp.bfloat16),
            jax.ShapeDtypeStruct((HEAD_DIM, half), jnp.float32),
            jax.ShapeDtypeStruct((HEAD_DIM, half), jnp.bfloat16),
        ),
        in_specs=[smem, smem] + [hbm] * 12,
        out_specs=(vmem, vmem, vmem),
        scratch_shapes=[
            pltpu.VMEM((2 * half, HEAD_DIM), jnp.bfloat16),
            pltpu.VMEM((2 * half, HEAD_DIM), jnp.bfloat16),
            pltpu.VMEM((half, HEAD_DIM), jnp.bfloat16),
            pltpu.VMEM((half, HEAD_DIM), jnp.bfloat16),
            pltpu.VMEM((HEAD_DIM, 2 * half), jnp.bfloat16),
            pltpu.VMEM((2 * half, QUERY_STEP), jnp.float32),
            pltpu.VMEM((2 * half, HEAD_DIM), jnp.float32),
            pltpu.SemaphoreType.DMA((24,)),
        ],
        compiler_params=pltpu.CompilerParams(vmem_limit_bytes=VMEM_BYTES),
        name="attention",
    )(starts, where, *kv_own, *kv_oth, *qg)


def shifted(x, axis, by):
    count = lax.axis_size(axis)
    return lax.ppermute(x, axis, [(i, (i + by) % count) for i in range(count)])


def near_ring(x, axis):
    return shifted(x, axis, 1), shifted(x, axis, -1)


def far_ring(below, above, axis):
    half = below.shape[0] // 2
    return shifted(below[:half], axis, 1), shifted(above[half:], axis, -1)


def heads_kernel(z_ref, *refs):
    sources, outs, sems = refs[:2], refs[2:6], refs[6]
    rows = sources[0].shape[0]
    copies = []
    for k, out in enumerate(outs):
        head = (z_ref[0] + k) % 4
        for n, source in enumerate(sources):
            copies.append(
                pltpu.make_async_copy(
                    source.at[:, pl.ds(pl.multiple_of(head * HEAD_DIM, HEAD_DIM), HEAD_DIM)],
                    out.at[pl.ds(n * rows, rows)], sems.at[len(copies)],
                )
            )
    for copy in copies:
        copy.start()
    for copy in copies:
        copy.wait()


def by_head(z, first, second):
    rows = first.shape[0]
    shape = jax.ShapeDtypeStruct((2 * rows, HEAD_DIM), first.dtype)
    hbm = pl.BlockSpec(memory_space=pl.ANY)
    vmem = pl.BlockSpec(memory_space=pltpu.VMEM)
    return pl.pallas_call(
        heads_kernel,
        out_shape=(shape,) * 4,
        in_specs=[pl.BlockSpec(memory_space=pltpu.SMEM), hbm, hbm],
        out_specs=(vmem,) * 4,
        scratch_shapes=[pltpu.SemaphoreType.DMA((8,))],
        name="by_head",
    )(z, first, second)


def swap_heads(parts):
    return parts[0], shifted(parts[1], "z", 1), shifted(parts[3], "z", -1), shifted(parts[2], "z", 2)


def stack_kernel(*refs):
    out, at = refs[-1], 0
    for part in refs[:-1]:
        out[at : at + part.shape[0], :] = part[...]
        at += part.shape[0]


def stacked(parts):
    rows = sum(p.shape[0] for p in parts)
    vmem = pl.BlockSpec(memory_space=pltpu.VMEM)
    return pl.pallas_call(
        stack_kernel,
        out_shape=jax.ShapeDtypeStruct((rows, *parts[0].shape[1:]), parts[0].dtype),
        in_specs=[vmem] * len(parts),
        out_specs=vmem,
        name="stack",
    )(*parts)


def factor_kernel(place, *refs, count, plan, blocks, aliased):
    n_pieces = len(refs) - 6 - aliased
    pieces, col_ref = refs[:n_pieces], refs[n_pieces]
    out, rows, cols, result, sems = refs[n_pieces + 1 + aliased :]
    x, z = place[0], place[1]
    block = HEAD_DIM
    copies = []

    def start(src, dst):
        copy = pltpu.make_async_copy(src, dst, sems.at[len(copies)])
        copy.start()
        copies.append(copy)

    line = 4 - (x // 2) * 2 - z // 2
    for n in range(8):
        at = ((n // 2 + line) % 4) * block
        start(col_ref.at[pl.ds(n * block, block)], cols.at[n % 2, pl.ds(pl.multiple_of(at, block), block)])
    targets, out_rows = plan(x, z)
    for piece, pair in zip(pieces, targets):
        for n, (which, local) in enumerate(pair):
            at = pl.multiple_of(local * block, block)
            start(piece.at[pl.ds(n * block, block)], rows.at[which, pl.ds(at, block)])
    for copy in copies:
        copy.wait()
    total = None
    for which in range(2):
        part = lax.dot_general(
            rows[which], cols[which], (((1,), (1,)), ((), ())), preferred_element_type=jnp.float32
        )
        total = part if total is None else total + part
    result[...] = total * (1.0 / count)
    stores = []
    for local in range(blocks):
        row = pl.multiple_of(out_rows[local] * block, block)
        store = pltpu.make_async_copy(
            result.at[pl.ds(local * block, block)], out.at[pl.ds(row, block)], sems.at[24 + local]
        )
        store.start()
        stores.append(store)
    for store in stores:
        store.wait()


def along_x_pieces(pieces):
    def plan(x, z):
        targets = [[((x + RING[outer]) % 4 // 2, slot) for slot in slots] for outer, slots in pieces]
        cols_at = (x + RING[pieces[0][0]]) % 2
        return targets, [cols_at * 4 + (z + RING[slot]) % 4 for slot in range(4)]

    return plan, 4


def along_z_pieces(pieces):
    groups = list(dict.fromkeys(outer for outer, _ in pieces))

    def plan(x, z):
        targets = []
        for outer, slots in pieces:
            at = [(x + RING[slot]) % 4 for slot in slots]
            targets.append([(xx // 2, groups.index(outer) * 2 + xx % 2) for xx in at])
        return targets, [c * 4 + (z + RING[g]) % 4 for g in groups for c in range(2)]

    return plan, 2 * len(groups)


def factor_part(place, groups, outers, cols, layout, count, name, into=None):
    held = []
    for outer in outers:
        held += [(3, (0, 1), groups[3]), (3, (2, 3), groups[4])] if outer == 3 else [(outer, (0, 1, 2, 3), groups[outer])]
    pieces = [piece for _, _, piece in held]
    plan, blocks = layout([(outer, slots) for outer, slots, _ in held])
    tokens = cols.shape[1]
    hbm = pl.BlockSpec(memory_space=pl.ANY)
    aliased = into is not None
    kernel = functools.partial(
        factor_kernel, count=count, plan=plan, blocks=blocks, aliased=int(aliased)
    )
    args = [place, *pieces, cols] + ([into] if aliased else [])
    return pl.pallas_call(
        kernel,
        out_shape=jax.ShapeDtypeStruct((8 * HEAD_DIM, 4 * HEAD_DIM), jnp.float32),
        in_specs=[pl.BlockSpec(memory_space=pltpu.SMEM)] + [hbm] * (len(args) - 1),
        out_specs=hbm,
        input_output_aliases={len(args) - 1: 0} if aliased else {},
        scratch_shapes=[
            pltpu.VMEM((2, blocks * HEAD_DIM, tokens), jnp.bfloat16),
            pltpu.VMEM((2, 4 * HEAD_DIM, tokens), jnp.bfloat16),
            pltpu.VMEM((blocks * HEAD_DIM, 4 * HEAD_DIM), jnp.float32),
            pltpu.SemaphoreType.DMA((32,)),
        ],
        compiler_params=pltpu.CompilerParams(vmem_limit_bytes=VMEM_BYTES),
        name=name,
    )(*args)


def column_moves():
    ranks = [(y, core, xh, z) for y in range(4) for core in range(2) for xh in range(2) for z in range(4)]
    place = {rank: n for n, rank in enumerate(ranks)}
    along_y, in_plane = [], []
    for y, core, xh, z in ranks:
        spread = (y + z) % 4
        along_y.append((place[y, core, xh, z], place[spread, core, xh, z]))
        in_plane.append((place[spread, core, xh, z], place[spread, xh, y // 2, (y % 2) * 2 + core]))
    return along_y, in_plane


def on_device(query_in, key_in, value_in, out_grads, doc_starts):
    all_tokens = query_in.shape[0] * 8
    xh, z = lax.axis_index("xh"), lax.axis_index("z")
    place = jnp.stack([lax.axis_index(X), z]).astype(jnp.int32)
    z_only = z.astype(jnp.int32)[None]
    kv_own = swap_heads(by_head(z_only, key_in, value_in))
    kv_oth = tuple(shifted(piece, "xh", 1) for piece in kv_own)
    qg = swap_heads(by_head(z_only, query_in, out_grads))
    where = jnp.stack([xh, z]).astype(jnp.int32)
    attended, near, far = attention(doc_starts, where, kv_own, kv_oth, qg)
    line = ("y", "core", "xh", "z")
    along_y, in_plane = column_moves()
    far = shifted(far, "xh", 1)
    a_near = near_ring(attended, "z")
    a_col = lax.ppermute(attended, line, along_y)
    near, far, attended, a_near, a_col = lax.optimization_barrier((near, far, attended, a_near, a_col))
    value_grads = (near + far).astype(jnp.bfloat16)
    g_near = near_ring(value_grads, X)
    g_col = lax.ppermute(value_grads, line, along_y)
    a_far = far_ring(*a_near, "z")
    a_col = lax.ppermute(a_col, line, in_plane)
    a_near, a_far, a_col, value_grads, g_near, g_col = lax.optimization_barrier(
        (a_near, a_far, a_col, value_grads, g_near, g_col)
    )
    group_a = stacked((attended, *a_near, *a_far))
    group_a, g_near, g_col = lax.optimization_barrier((group_a, g_near, g_col))
    a_near = near_ring(group_a, X)
    g_far = far_ring(*g_near, X)
    g_col = lax.ppermute(g_col, line, in_plane)
    cols_a = lax.all_gather(a_col, ("y", "core"), axis=0, tiled=True)
    group_g = stacked((value_grads, *g_near, *g_far))
    g_near = near_ring(group_g, "z")
    g_col, _ = lax.optimization_barrier((g_col, group_g))
    cols_g = lax.all_gather(g_col, ("y", "core"), axis=0, tiled=True)
    a_far = far_ring(*a_near, X)
    g_far = far_ring(*g_near, "z")
    rows_a, rows_g = (group_a, *a_near, *a_far), (group_g, *g_near, *g_far)
    input_factor = factor_part(place, rows_a, (1, 2), cols_a, along_x_pieces, all_tokens, "input_near")
    grad_factor = factor_part(place, rows_g, (0, 1, 2), cols_g, along_z_pieces, all_tokens, "grad_near")
    input_factor, grad_factor = lax.optimization_barrier((input_factor, grad_factor))
    input_factor = factor_part(
        place, rows_a, (0, 3), cols_a, along_x_pieces, all_tokens, "input_far", input_factor
    )
    grad_factor = factor_part(
        place, rows_g, (3,), cols_g, along_z_pieces, all_tokens, "grad_far", grad_factor
    )
    return (input_factor, grad_factor)


def solution(mesh):
    split = Mesh(mesh.devices.reshape(4, 2, 2, 4, 2), ("y", "core", "xh", "z", "xl"))
    tokens, features = ("xh", "z"), ("y", "core", "xl")
    spec = P(tokens, features)
    out = P(("y", "core"), ("xh", "z", "xl"))
    return jax.shard_map(
        on_device, mesh=split, in_specs=(spec, spec, spec, spec, P()), out_specs=(out, out),
        check_vma=False,
    )
```

```python
import functools
import math

import jax
import jax.numpy as jnp
from jax import lax
from jax.experimental import pallas as pl
from jax.experimental.pallas import tpu as pltpu
from jax.sharding import Mesh
from jax.sharding import PartitionSpec as P

HEAD_DIM = 128
X = ("xh", "xl")
RING = (0, 3, 1, 2)
MASK_FLOOR = -1e30
KEY_STEP = 512
QUERY_STEP = 512
VMEM_BYTES = 56 * 1024 * 1024


def attention_kernel(starts, where_ref, *refs):
    kv_own, kv_oth, qg = refs[:4], refs[4:8], refs[8:12]
    att_ref, near_ref, far_ref = refs[12:15]
    k_all, v_all, q_ref, g_ref, v_turned, scores, grads, sems = refs[15:]
    half = q_ref.shape[0]
    part = half // 4
    half_id, z = where_ref[0], where_ref[1]
    own_at = pl.multiple_of(half_id * half, half)
    oth_at = pl.multiple_of((1 - half_id) * half, half)
    copies = []
    for pieces, base, targets in (
        (kv_own, own_at, (k_all, v_all)), (kv_oth, oth_at, (k_all, v_all)), (qg, 0, (q_ref, g_ref))
    ):
        for step, piece in zip(RING, pieces):
            at = pl.multiple_of(base + ((z + step) % 4) * part, part)
            for n, target in enumerate(targets):
                copies.append(
                    pltpu.make_async_copy(
                        piece.at[pl.ds(n * part, part)], target.at[pl.ds(at, part)], sems.at[len(copies)]
                    )
                )
    for copy in copies:
        copy.start()
    grads[...] = jnp.zeros_like(grads)
    for copy in copies:
        copy.wait()
    all_tokens = 2 * half
    docs = starts.shape[0]
    for at in range(0, all_tokens, KEY_STEP):
        v_turned[:, at : at + KEY_STEP] = v_all[at : at + KEY_STEP, :].T
    scale = math.log2(math.e) / math.sqrt(HEAD_DIM)
    groups = KEY_STEP // 8

    def query_block(block, carry):
        row = pl.multiple_of(block * QUERY_STEP, QUERY_STEP)
        first = own_at + row
        last = first + QUERY_STEP - 1
        pos = first + lax.broadcasted_iota(jnp.int32, (1, QUERY_STEP), 1)
        begin = jnp.zeros((1, QUERY_STEP), jnp.int32)
        finish = jnp.full((1, QUERY_STEP), all_tokens, jnp.int32)
        lowest, latest = jnp.int32(0), jnp.int32(0)
        highest, soonest = jnp.int32(all_tokens), jnp.int32(all_tokens)
        for d in range(docs):
            start = starts[d]
            lowest = jnp.where(start <= first, jnp.maximum(lowest, start), lowest)
            highest = jnp.where(start > last, jnp.minimum(highest, start), highest)
            latest = jnp.where(start <= last, jnp.maximum(latest, start), latest)
            soonest = jnp.where(start > first, jnp.minimum(soonest, start), soonest)
            begin = jnp.where(start <= pos, jnp.maximum(begin, start), begin)
            finish = jnp.where(start > pos, jnp.minimum(finish, start), finish)
        step_from = lowest // KEY_STEP
        step_to = (highest + KEY_STEP - 1) // KEY_STEP
        inside_from = jnp.minimum((latest + KEY_STEP - 1) // KEY_STEP, step_to)
        inside_to = jnp.maximum(soonest // KEY_STEP, inside_from)
        queries = q_ref[pl.ds(row, QUERY_STEP), :]
        cotangents = g_ref[pl.ds(row, QUERY_STEP), :]
        key_iota = lax.broadcasted_iota(jnp.int32, (KEY_STEP, QUERY_STEP), 0)

        def score_step(step, peak, masked):
            at = pl.multiple_of(step * KEY_STEP, KEY_STEP)
            s = lax.dot_general(
                k_all[pl.ds(at, KEY_STEP), :], queries, (((1,), (1,)), ((), ())),
                preferred_element_type=jnp.float32,
            ) * scale
            if masked:
                allowed = (key_iota >= begin - at) & (key_iota < finish - at)
                s = jnp.where(allowed, s, MASK_FLOOR)
            scores[pl.ds(at, KEY_STEP), :] = s
            return jnp.maximum(peak, jnp.max(s.reshape(groups, 8, QUERY_STEP), axis=0))

        edge_step = functools.partial(score_step, masked=True)
        inside_step = functools.partial(score_step, masked=False)
        peak = jnp.full((8, QUERY_STEP), MASK_FLOOR, jnp.float32)
        peak = lax.fori_loop(step_from, inside_from, edge_step, peak)
        peak = lax.fori_loop(inside_from, inside_to, inside_step, peak)
        peak = lax.fori_loop(inside_to, step_to, edge_step, peak)
        peak = jnp.max(peak, axis=0, keepdims=True)

        def mass_step(step, mass):
            at = pl.multiple_of(step * KEY_STEP, KEY_STEP)
            e = jnp.exp2(scores[pl.ds(at, KEY_STEP), :] - peak)
            scores[pl.ds(at, KEY_STEP), :] = e
            return mass + jnp.sum(e.reshape(groups, 8, QUERY_STEP), axis=0)

        mass = lax.fori_loop(step_from, step_to, mass_step, jnp.zeros((8, QUERY_STEP), jnp.float32))
        share = 1.0 / jnp.sum(mass, axis=0, keepdims=True)

        def value_step(step, summed):
            at = pl.multiple_of(step * KEY_STEP, KEY_STEP)
            w = (scores[pl.ds(at, KEY_STEP), :] * share).astype(jnp.bfloat16)
            grads[pl.ds(at, KEY_STEP), :] += jnp.dot(
                w, cotangents, preferred_element_type=jnp.float32
            )
            return summed + jnp.dot(
                v_turned[:, pl.ds(at, KEY_STEP)], w, preferred_element_type=jnp.float32
            )

        summed = lax.fori_loop(
            step_from, step_to, value_step, jnp.zeros((HEAD_DIM, QUERY_STEP), jnp.float32)
        )
        att_ref[:, pl.ds(row, QUERY_STEP)] = summed.astype(jnp.bfloat16)
        return carry

    lax.fori_loop(0, half // QUERY_STEP, query_block, 0)
    for at in range(0, half, KEY_STEP):
        near_ref[:, at : at + KEY_STEP] = grads[pl.ds(own_at + at, KEY_STEP), :].T
        far_ref[:, at : at + KEY_STEP] = grads[pl.ds(oth_at + at, KEY_STEP), :].T.astype(jnp.bfloat16)


def attention(starts, where, kv_own, kv_oth, qg):
    half = 2 * qg[0].shape[0]
    hbm = pl.BlockSpec(memory_space=pl.ANY)
    vmem = pl.BlockSpec(memory_space=pltpu.VMEM)
    smem = pl.BlockSpec(memory_space=pltpu.SMEM)
    return pl.pallas_call(
        attention_kernel,
        out_shape=(
            jax.ShapeDtypeStruct((HEAD_DIM, half), jnp.bfloat16),
            jax.ShapeDtypeStruct((HEAD_DIM, half), jnp.float32),
            jax.ShapeDtypeStruct((HEAD_DIM, half), jnp.bfloat16),
        ),
        in_specs=[smem, smem] + [hbm] * 12,
        out_specs=(vmem, vmem, vmem),
        scratch_shapes=[
            pltpu.VMEM((2 * half, HEAD_DIM), jnp.bfloat16),
            pltpu.VMEM((2 * half, HEAD_DIM), jnp.bfloat16),
            pltpu.VMEM((half, HEAD_DIM), jnp.bfloat16),
            pltpu.VMEM((half, HEAD_DIM), jnp.bfloat16),
            pltpu.VMEM((HEAD_DIM, 2 * half), jnp.bfloat16),
            pltpu.VMEM((2 * half, QUERY_STEP), jnp.float32),
            pltpu.VMEM((2 * half, HEAD_DIM), jnp.float32),
            pltpu.SemaphoreType.DMA((24,)),
        ],
        compiler_params=pltpu.CompilerParams(vmem_limit_bytes=VMEM_BYTES),
        name="attention",
    )(starts, where, *kv_own, *kv_oth, *qg)


def shifted(x, axis, by):
    count = lax.axis_size(axis)
    return lax.ppermute(x, axis, [(i, (i + by) % count) for i in range(count)])


def near_ring(x, axis):
    return shifted(x, axis, 1), shifted(x, axis, -1)


def heads_kernel(z_ref, *refs):
    sources, outs, sems = refs[:2], refs[2:6], refs[6]
    rows = sources[0].shape[0]
    copies = []
    for k, out in enumerate(outs):
        head = (z_ref[0] + k) % 4
        for n, source in enumerate(sources):
            copies.append(
                pltpu.make_async_copy(
                    source.at[:, pl.ds(pl.multiple_of(head * HEAD_DIM, HEAD_DIM), HEAD_DIM)],
                    out.at[pl.ds(n * rows, rows)], sems.at[len(copies)],
                )
            )
    for copy in copies:
        copy.start()
    for copy in copies:
        copy.wait()


def by_head(z, first, second):
    rows = first.shape[0]
    shape = jax.ShapeDtypeStruct((2 * rows, HEAD_DIM), first.dtype)
    hbm = pl.BlockSpec(memory_space=pl.ANY)
    vmem = pl.BlockSpec(memory_space=pltpu.VMEM)
    return pl.pallas_call(
        heads_kernel,
        out_shape=(shape,) * 4,
        in_specs=[pl.BlockSpec(memory_space=pltpu.SMEM), hbm, hbm],
        out_specs=(vmem,) * 4,
        scratch_shapes=[pltpu.SemaphoreType.DMA((8,))],
        name="by_head",
    )(z, first, second)


def swap_heads(parts):
    return parts[0], shifted(parts[1], "z", 1), shifted(parts[3], "z", -1), shifted(parts[2], "z", 2)


def stack_kernel(*refs):
    out, at = refs[-1], 0
    for part in refs[:-1]:
        out[at : at + part.shape[0], :] = part[...]
        at += part.shape[0]


def stacked(parts):
    rows = sum(p.shape[0] for p in parts)
    vmem = pl.BlockSpec(memory_space=pltpu.VMEM)
    return pl.pallas_call(
        stack_kernel,
        out_shape=jax.ShapeDtypeStruct((rows, *parts[0].shape[1:]), parts[0].dtype),
        in_specs=[vmem] * len(parts),
        out_specs=vmem,
        name="stack",
    )(*parts)


def factors_kernel(place, *refs, count, jobs, aliased):
    n_in = sum(job[0] + 1 for job in jobs)
    refs = list(refs)
    inputs, refs = refs[:n_in], refs[n_in + 2 * aliased :]
    outs, scratch = refs[: len(jobs)], refs[len(jobs) :]
    x, z = place[0], place[1]
    block = HEAD_DIM
    line = 8 - (x // 2) * 2 - z // 2 - 2 * (z % 2)
    waits, out_rows = [], []
    for j, (n_pieces, plan, _) in enumerate(jobs):
        rows, cols, sems = scratch[4 * j], scratch[4 * j + 1], scratch[4 * j + 3]
        pieces, col_ref = inputs[:n_pieces], inputs[n_pieces]
        inputs = inputs[n_pieces + 1 :]
        copies = []
        for n in range(8):
            at = pl.multiple_of(((n // 2 + line) % 4) * block, block)
            copies.append((col_ref.at[pl.ds(n * block, block)], cols.at[n % 2, pl.ds(at, block)]))
        targets, to = plan(x, z)
        for piece, pair in zip(pieces, targets):
            for n, (which, local) in enumerate(pair):
                at = pl.multiple_of(local * block, block)
                copies.append((piece.at[pl.ds(n * block, block)], rows.at[which, pl.ds(at, block)]))
        waits.append([pltpu.make_async_copy(src, dst, sems.at[k]) for k, (src, dst) in enumerate(copies)])
        out_rows.append(to)
        for copy in waits[-1]:
            copy.start()
    stores = []
    for j, (_, _, blocks) in enumerate(jobs):
        rows, cols, result, sems = scratch[4 * j : 4 * j + 4]
        for copy in waits[j]:
            copy.wait()
        total = None
        for which in range(2):
            part = lax.dot_general(
                rows[which], cols[which], (((1,), (1,)), ((), ())), preferred_element_type=jnp.float32
            )
            total = part if total is None else total + part
        result[...] = total * (1.0 / count)
        for local in range(blocks):
            row = pl.multiple_of(out_rows[j][local] * block, block)
            store = pltpu.make_async_copy(
                result.at[pl.ds(local * block, block)], outs[j].at[pl.ds(row, block)], sems.at[24 + local]
            )
            store.start()
            stores.append(store)
    for store in stores:
        store.wait()


def along_x_pieces(pieces):
    def plan(x, z):
        targets = [[((x + RING[outer]) % 4 // 2, slot) for slot in slots] for outer, slots in pieces]
        cols_at = (x + RING[pieces[0][0]]) % 2
        return targets, [cols_at * 4 + (z + RING[slot]) % 4 for slot in range(4)]

    return plan, 4


def along_z_pieces(pieces):
    groups = list(dict.fromkeys(outer for outer, _ in pieces))

    def plan(x, z):
        targets = []
        for outer, slots in pieces:
            at = [(x + RING[slot]) % 4 for slot in slots]
            targets.append([(xx // 2, groups.index(outer) * 2 + xx % 2) for xx in at])
        return targets, [c * 4 + (z + RING[g]) % 4 for g in groups for c in range(2)]

    return plan, 2 * len(groups)


def halved(groups):
    return [(outer, slots, groups[outer][n]) for outer in range(4) for n, slots in enumerate(((0, 1), (2, 3)))]


def factors_part(place, jobs, count, name, into=()):
    args, plans, scratch = [place], [], []
    for pieces, outers, cols, layout in jobs:
        held = [piece for piece in pieces if piece[0] in outers]
        plan, blocks = layout([(outer, slots) for outer, slots, _ in held])
        args += [array for _, _, array in held] + [cols]
        plans.append((len(held), plan, blocks))
        scratch += [
            pltpu.VMEM((2, blocks * HEAD_DIM, cols.shape[1]), jnp.bfloat16),
            pltpu.VMEM((2, 4 * HEAD_DIM, cols.shape[1]), jnp.bfloat16),
            pltpu.VMEM((blocks * HEAD_DIM, 4 * HEAD_DIM), jnp.float32),
            pltpu.SemaphoreType.DMA((32,)),
        ]
    hbm = pl.BlockSpec(memory_space=pl.ANY)
    aliased = len(into) > 0
    kernel = functools.partial(factors_kernel, count=count, jobs=plans, aliased=int(aliased))
    shape = jax.ShapeDtypeStruct((8 * HEAD_DIM, 4 * HEAD_DIM), jnp.float32)
    return pl.pallas_call(
        kernel,
        out_shape=(shape, shape),
        in_specs=[pl.BlockSpec(memory_space=pltpu.SMEM)] + [hbm] * (len(args) + len(into) - 1),
        out_specs=(hbm, hbm),
        input_output_aliases={len(args): 0, len(args) + 1: 1} if aliased else {},
        scratch_shapes=scratch,
        compiler_params=pltpu.CompilerParams(vmem_limit_bytes=VMEM_BYTES),
        name=name,
    )(*args, *into)


def column_moves():
    ranks = [(y, core, xh, z) for y in range(4) for core in range(2) for xh in range(2) for z in range(4)]
    place = {rank: n for n, rank in enumerate(ranks)}
    along_y, in_plane = [], []
    for y, core, xh, z in ranks:
        spread = (y + z + 2 * core) % 4
        along_y.append((place[y, core, xh, z], place[spread, core, xh, z]))
        in_plane.append((place[spread, core, xh, z], place[spread, xh, y // 2, (y % 2) * 2 + core]))
    return along_y, in_plane


def on_device(query_in, key_in, value_in, out_grads, doc_starts):
    all_tokens = query_in.shape[0] * 8
    xh, z = lax.axis_index("xh"), lax.axis_index("z")
    place = jnp.stack([lax.axis_index(X), z]).astype(jnp.int32)
    z_only = z.astype(jnp.int32)[None]
    kv_parts = by_head(z_only, key_in, value_in)
    kv_parts, query_in, out_grads = lax.optimization_barrier((kv_parts, query_in, out_grads))
    kv_own = swap_heads(kv_parts)
    kv_oth = tuple(shifted(piece, "xh", 1) for piece in kv_own)
    qg = swap_heads(by_head(z_only, query_in, out_grads))
    where = jnp.stack([xh, z]).astype(jnp.int32)
    attended, near, far = attention(doc_starts, where, kv_own, kv_oth, qg)
    line = ("y", "core", "xh", "z")
    along_y, in_plane = column_moves()
    far = shifted(far, "xh", 1)
    a_near = near_ring(attended, "z")
    a_col = lax.ppermute(attended, line, along_y)
    near, far, attended, a_near, a_col = lax.optimization_barrier((near, far, attended, a_near, a_col))
    value_grads = (near + far).astype(jnp.bfloat16)
    g_near = near_ring(value_grads, X)
    g_far = shifted(value_grads, X, 2)
    g_col = lax.ppermute(lax.ppermute(value_grads, line, along_y), line, in_plane)
    a_far = shifted(attended, "z", 2)
    a_col = lax.ppermute(a_col, line, in_plane)
    a_first, a_second = stacked((attended, a_near[0])), stacked((a_near[1], a_far))
    g_first, g_second = stacked((value_grads, g_near[0])), stacked((g_near[1], g_far))
    a_first, a_second, a_col, g_first, g_second, g_col = lax.optimization_barrier(
        (a_first, a_second, a_col, g_first, g_second, g_col)
    )
    cols_a = lax.all_gather(a_col, ("y", "core"), axis=0, tiled=True)
    cols_g = lax.all_gather(g_col, ("y", "core"), axis=0, tiled=True)
    a_firsts, g_firsts = near_ring(a_first, X), near_ring(g_first, "z")
    a_firsts, g_firsts, a_second, g_second = lax.optimization_barrier((a_firsts, g_firsts, a_second, g_second))
    a_seconds, g_seconds = near_ring(a_second, X), near_ring(g_second, "z")
    a_firsts, g_firsts, a_seconds, g_seconds = lax.optimization_barrier((a_firsts, g_firsts, a_seconds, g_seconds))
    a_far = shifted(a_firsts[0], X, 1), shifted(a_seconds[1], X, -1)
    g_far = shifted(g_firsts[0], "z", 1), shifted(g_seconds[1], "z", -1)
    rows_a = halved(((a_first, a_second), *zip(a_firsts, a_seconds), a_far))
    rows_g = halved(((g_first, g_second), *zip(g_firsts, g_seconds), g_far))
    near = ((rows_a, (1, 2), cols_a, along_x_pieces), (rows_g, (0, 1, 2), cols_g, along_z_pieces))
    far = ((rows_a, (0, 3), cols_a, along_x_pieces), (rows_g, (3,), cols_g, along_z_pieces))
    factors = factors_part(place, near, all_tokens, "near_rows")
    return factors_part(place, far, all_tokens, "far_rows", factors)


def solution(mesh):
    split = Mesh(mesh.devices.reshape(4, 2, 2, 4, 2), ("y", "core", "xh", "z", "xl"))
    tokens, features = ("xh", "z"), ("y", "core", "xl")
    spec = P(tokens, features)
    out = P(("y", "core"), ("xh", "z", "xl"))
    return jax.shard_map(
        on_device, mesh=split, in_specs=(spec, spec, spec, spec, P()), out_specs=(out, out),
        check_vma=False,
    )
```

```python
import functools
import math

import jax
import jax.numpy as jnp
from jax import lax
from jax.experimental import pallas as pl
from jax.experimental.pallas import tpu as pltpu
from jax.sharding import Mesh
from jax.sharding import PartitionSpec as P

HEAD_DIM = 128
X = ("xh", "xl")
RING = (0, 3, 1, 2)
MASK_FLOOR = -1e30
KEY_STEP = 512
QUERY_STEP = 512
VMEM_BYTES = 56 * 1024 * 1024


def attention_kernel(starts, where_ref, *refs):
    kv_own, kv_oth, qg = refs[:4], refs[4:8], refs[8:12]
    att_ref, near_ref, far_ref = refs[12:15]
    k_all, v_all, q_ref, g_ref, v_turned, scores, grads, sems = refs[15:]
    half = q_ref.shape[0]
    part = half // 4
    half_id, z = where_ref[0], where_ref[1]
    own_at = pl.multiple_of(half_id * half, half)
    oth_at = pl.multiple_of((1 - half_id) * half, half)
    copies = []
    for pieces, base, targets in (
        (kv_own, own_at, (k_all, v_all)), (kv_oth, oth_at, (k_all, v_all)), (qg, 0, (q_ref, g_ref))
    ):
        for step, piece in zip(RING, pieces):
            at = pl.multiple_of(base + ((z + step) % 4) * part, part)
            for n, target in enumerate(targets):
                copies.append(
                    pltpu.make_async_copy(
                        piece.at[pl.ds(n * part, part)], target.at[pl.ds(at, part)], sems.at[len(copies)]
                    )
                )
    for copy in copies:
        copy.start()
    grads[...] = jnp.zeros_like(grads)
    for copy in copies:
        copy.wait()
    all_tokens = 2 * half
    docs = starts.shape[0]
    for at in range(0, all_tokens, KEY_STEP):
        v_turned[:, at : at + KEY_STEP] = v_all[at : at + KEY_STEP, :].T
    scale = math.log2(math.e) / math.sqrt(HEAD_DIM)
    groups = KEY_STEP // 8

    def query_block(block, carry):
        row = pl.multiple_of(block * QUERY_STEP, QUERY_STEP)
        first = own_at + row
        last = first + QUERY_STEP - 1
        pos = first + lax.broadcasted_iota(jnp.int32, (1, QUERY_STEP), 1)
        begin = jnp.zeros((1, QUERY_STEP), jnp.int32)
        finish = jnp.full((1, QUERY_STEP), all_tokens, jnp.int32)
        lowest, latest = jnp.int32(0), jnp.int32(0)
        highest, soonest = jnp.int32(all_tokens), jnp.int32(all_tokens)
        for d in range(docs):
            start = starts[d]
            lowest = jnp.where(start <= first, jnp.maximum(lowest, start), lowest)
            highest = jnp.where(start > last, jnp.minimum(highest, start), highest)
            latest = jnp.where(start <= last, jnp.maximum(latest, start), latest)
            soonest = jnp.where(start > first, jnp.minimum(soonest, start), soonest)
            begin = jnp.where(start <= pos, jnp.maximum(begin, start), begin)
            finish = jnp.where(start > pos, jnp.minimum(finish, start), finish)
        step_from = lowest // KEY_STEP
        step_to = (highest + KEY_STEP - 1) // KEY_STEP
        inside_from = jnp.minimum((latest + KEY_STEP - 1) // KEY_STEP, step_to)
        inside_to = jnp.maximum(soonest // KEY_STEP, inside_from)
        queries = q_ref[pl.ds(row, QUERY_STEP), :]
        cotangents = g_ref[pl.ds(row, QUERY_STEP), :]
        key_iota = lax.broadcasted_iota(jnp.int32, (KEY_STEP, QUERY_STEP), 0)

        def score_step(step, peak, masked):
            at = pl.multiple_of(step * KEY_STEP, KEY_STEP)
            s = lax.dot_general(
                k_all[pl.ds(at, KEY_STEP), :], queries, (((1,), (1,)), ((), ())),
                preferred_element_type=jnp.float32,
            ) * scale
            if masked:
                allowed = (key_iota >= begin - at) & (key_iota < finish - at)
                s = jnp.where(allowed, s, MASK_FLOOR)
            scores[pl.ds(at, KEY_STEP), :] = s
            return jnp.maximum(peak, jnp.max(s.reshape(groups, 8, QUERY_STEP), axis=0))

        edge_step = functools.partial(score_step, masked=True)
        inside_step = functools.partial(score_step, masked=False)
        peak = jnp.full((8, QUERY_STEP), MASK_FLOOR, jnp.float32)
        peak = lax.fori_loop(step_from, inside_from, edge_step, peak)
        peak = lax.fori_loop(inside_from, inside_to, inside_step, peak)
        peak = lax.fori_loop(inside_to, step_to, edge_step, peak)
        peak = jnp.max(peak, axis=0, keepdims=True)

        def mass_step(step, mass):
            at = pl.multiple_of(step * KEY_STEP, KEY_STEP)
            e = jnp.exp2(scores[pl.ds(at, KEY_STEP), :] - peak)
            scores[pl.ds(at, KEY_STEP), :] = e
            return mass + jnp.sum(e.reshape(groups, 8, QUERY_STEP), axis=0)

        mass = lax.fori_loop(step_from, step_to, mass_step, jnp.zeros((8, QUERY_STEP), jnp.float32))
        share = 1.0 / jnp.sum(mass, axis=0, keepdims=True)

        def value_step(step, summed):
            at = pl.multiple_of(step * KEY_STEP, KEY_STEP)
            w = (scores[pl.ds(at, KEY_STEP), :] * share).astype(jnp.bfloat16)
            grads[pl.ds(at, KEY_STEP), :] += jnp.dot(
                w, cotangents, preferred_element_type=jnp.float32
            )
            return summed + jnp.dot(
                v_turned[:, pl.ds(at, KEY_STEP)], w, preferred_element_type=jnp.float32
            )

        summed = lax.fori_loop(
            step_from, step_to, value_step, jnp.zeros((HEAD_DIM, QUERY_STEP), jnp.float32)
        )
        att_ref[:, pl.ds(row, QUERY_STEP)] = summed.astype(jnp.bfloat16)
        return carry

    lax.fori_loop(0, half // QUERY_STEP, query_block, 0)
    for at in range(0, half, KEY_STEP):
        near_ref[:, at : at + KEY_STEP] = grads[pl.ds(own_at + at, KEY_STEP), :].T
        far_ref[:, at : at + KEY_STEP] = grads[pl.ds(oth_at + at, KEY_STEP), :].T.astype(jnp.bfloat16)


def attention(starts, where, kv_own, kv_oth, qg):
    half = 2 * qg[0].shape[0]
    hbm = pl.BlockSpec(memory_space=pl.ANY)
    vmem = pl.BlockSpec(memory_space=pltpu.VMEM)
    smem = pl.BlockSpec(memory_space=pltpu.SMEM)
    return pl.pallas_call(
        attention_kernel,
        out_shape=(
            jax.ShapeDtypeStruct((HEAD_DIM, half), jnp.bfloat16),
            jax.ShapeDtypeStruct((HEAD_DIM, half), jnp.float32),
            jax.ShapeDtypeStruct((HEAD_DIM, half), jnp.bfloat16),
        ),
        in_specs=[smem, smem] + [hbm] * 12,
        out_specs=(vmem, vmem, vmem),
        scratch_shapes=[
            pltpu.VMEM((2 * half, HEAD_DIM), jnp.bfloat16),
            pltpu.VMEM((2 * half, HEAD_DIM), jnp.bfloat16),
            pltpu.VMEM((half, HEAD_DIM), jnp.bfloat16),
            pltpu.VMEM((half, HEAD_DIM), jnp.bfloat16),
            pltpu.VMEM((HEAD_DIM, 2 * half), jnp.bfloat16),
            pltpu.VMEM((2 * half, QUERY_STEP), jnp.float32),
            pltpu.VMEM((2 * half, HEAD_DIM), jnp.float32),
            pltpu.SemaphoreType.DMA((24,)),
        ],
        compiler_params=pltpu.CompilerParams(vmem_limit_bytes=VMEM_BYTES),
        name="attention",
    )(starts, where, *kv_own, *kv_oth, *qg)


def shifted(x, axis, by):
    count = lax.axis_size(axis)
    return lax.ppermute(x, axis, [(i, (i + by) % count) for i in range(count)])


def near_ring(x, axis):
    return shifted(x, axis, 1), shifted(x, axis, -1)


def heads_kernel(z_ref, *refs):
    sources, outs, sems = refs[:2], refs[2:6], refs[6]
    rows = sources[0].shape[0]
    copies = []
    for k, out in enumerate(outs):
        head = (z_ref[0] + k) % 4
        for n, source in enumerate(sources):
            copies.append(
                pltpu.make_async_copy(
                    source.at[:, pl.ds(pl.multiple_of(head * HEAD_DIM, HEAD_DIM), HEAD_DIM)],
                    out.at[pl.ds(n * rows, rows)], sems.at[len(copies)],
                )
            )
    for copy in copies:
        copy.start()
    for copy in copies:
        copy.wait()


def by_head(z, first, second):
    rows = first.shape[0]
    shape = jax.ShapeDtypeStruct((2 * rows, HEAD_DIM), first.dtype)
    hbm = pl.BlockSpec(memory_space=pl.ANY)
    vmem = pl.BlockSpec(memory_space=pltpu.VMEM)
    return pl.pallas_call(
        heads_kernel,
        out_shape=(shape,) * 4,
        in_specs=[pl.BlockSpec(memory_space=pltpu.SMEM), hbm, hbm],
        out_specs=(vmem,) * 4,
        scratch_shapes=[pltpu.SemaphoreType.DMA((8,))],
        name="by_head",
    )(z, first, second)


def swap_heads(parts):
    return parts[0], shifted(parts[1], "z", 1), shifted(parts[3], "z", -1), shifted(parts[2], "z", 2)


def stack_kernel(*refs):
    out, at = refs[-1], 0
    for part in refs[:-1]:
        out[at : at + part.shape[0], :] = part[...]
        at += part.shape[0]


def stacked(parts):
    rows = sum(p.shape[0] for p in parts)
    vmem = pl.BlockSpec(memory_space=pltpu.VMEM)
    return pl.pallas_call(
        stack_kernel,
        out_shape=jax.ShapeDtypeStruct((rows, *parts[0].shape[1:]), parts[0].dtype),
        in_specs=[vmem] * len(parts),
        out_specs=vmem,
        name="stack",
    )(*parts)


def factors_kernel(place, *refs, count, jobs, aliased):
    n_in = sum(job[0] + 1 for job in jobs)
    refs = list(refs)
    inputs, refs = refs[:n_in], refs[n_in + 2 * aliased :]
    outs, scratch = refs[: len(jobs)], refs[len(jobs) :]
    x, z = place[0], place[1]
    block = HEAD_DIM
    line = 8 - (x // 2) * 2 - z // 2 - 2 * (z % 2)
    waits, out_rows = [], []
    for j, (n_pieces, plan, _) in enumerate(jobs):
        rows, cols, sems = scratch[4 * j], scratch[4 * j + 1], scratch[4 * j + 3]
        pieces, col_ref = inputs[:n_pieces], inputs[n_pieces]
        inputs = inputs[n_pieces + 1 :]
        copies = []
        for n in range(8):
            at = pl.multiple_of(((n // 2 + line) % 4) * block, block)
            copies.append((col_ref.at[pl.ds(n * block, block)], cols.at[n % 2, pl.ds(at, block)]))
        targets, to = plan(x, z)
        for piece, pair in zip(pieces, targets):
            for n, (which, local) in enumerate(pair):
                at = pl.multiple_of(local * block, block)
                copies.append((piece.at[pl.ds(n * block, block)], rows.at[which, pl.ds(at, block)]))
        waits.append([pltpu.make_async_copy(src, dst, sems.at[k]) for k, (src, dst) in enumerate(copies)])
        out_rows.append(to)
        for copy in waits[-1]:
            copy.start()
    stores = []
    for j, (_, _, blocks) in enumerate(jobs):
        rows, cols, result, sems = scratch[4 * j : 4 * j + 4]
        for copy in waits[j]:
            copy.wait()
        total = None
        for which in range(2):
            part = lax.dot_general(
                rows[which], cols[which], (((1,), (1,)), ((), ())), preferred_element_type=jnp.float32
            )
            total = part if total is None else total + part
        result[...] = total * (1.0 / count)
        for local in range(blocks):
            row = pl.multiple_of(out_rows[j][local] * block, block)
            store = pltpu.make_async_copy(
                result.at[pl.ds(local * block, block)], outs[j].at[pl.ds(row, block)], sems.at[24 + local]
            )
            store.start()
            stores.append(store)
    for store in stores:
        store.wait()


def along_x_pieces(pieces):
    def plan(x, z):
        targets = [[((x + RING[outer]) % 4 // 2, slot) for slot in slots] for outer, slots in pieces]
        cols_at = (x + RING[pieces[0][0]]) % 2
        return targets, [cols_at * 4 + (z + RING[slot]) % 4 for slot in range(4)]

    return plan, 4


def along_z_pieces(pieces):
    groups = list(dict.fromkeys(outer for outer, _ in pieces))

    def plan(x, z):
        targets = []
        for outer, slots in pieces:
            at = [(x + RING[slot]) % 4 for slot in slots]
            targets.append([(xx // 2, groups.index(outer) * 2 + xx % 2) for xx in at])
        return targets, [c * 4 + (z + RING[g]) % 4 for g in groups for c in range(2)]

    return plan, 2 * len(groups)


def halved(groups):
    return [(outer, slots, groups[outer][n]) for outer in range(4) for n, slots in enumerate(((0, 1), (2, 3)))]


def factors_part(place, jobs, count, name, into=()):
    args, plans, scratch = [place], [], []
    for pieces, outers, cols, layout in jobs:
        held = [piece for piece in pieces if piece[0] in outers]
        plan, blocks = layout([(outer, slots) for outer, slots, _ in held])
        args += [array for _, _, array in held] + [cols]
        plans.append((len(held), plan, blocks))
        scratch += [
            pltpu.VMEM((2, blocks * HEAD_DIM, cols.shape[1]), jnp.bfloat16),
            pltpu.VMEM((2, 4 * HEAD_DIM, cols.shape[1]), jnp.bfloat16),
            pltpu.VMEM((blocks * HEAD_DIM, 4 * HEAD_DIM), jnp.float32),
            pltpu.SemaphoreType.DMA((32,)),
        ]
    hbm = pl.BlockSpec(memory_space=pl.ANY)
    aliased = len(into) > 0
    kernel = functools.partial(factors_kernel, count=count, jobs=plans, aliased=int(aliased))
    shape = jax.ShapeDtypeStruct((8 * HEAD_DIM, 4 * HEAD_DIM), jnp.float32)
    return pl.pallas_call(
        kernel,
        out_shape=(shape, shape),
        in_specs=[pl.BlockSpec(memory_space=pltpu.SMEM)] + [hbm] * (len(args) + len(into) - 1),
        out_specs=(hbm, hbm),
        input_output_aliases={len(args): 0, len(args) + 1: 1} if aliased else {},
        scratch_shapes=scratch,
        compiler_params=pltpu.CompilerParams(vmem_limit_bytes=VMEM_BYTES),
        name=name,
    )(*args, *into)


def column_moves():
    ranks = [(y, core, xh, z) for y in range(4) for core in range(2) for xh in range(2) for z in range(4)]
    place = {rank: n for n, rank in enumerate(ranks)}
    along_y, in_plane = [], []
    for y, core, xh, z in ranks:
        spread = (y + z + 2 * core) % 4
        along_y.append((place[y, core, xh, z], place[spread, core, xh, z]))
        in_plane.append((place[spread, core, xh, z], place[spread, xh, y // 2, (y % 2) * 2 + core]))
    return along_y, in_plane


def on_device(query_in, key_in, value_in, out_grads, doc_starts):
    all_tokens = query_in.shape[0] * 8
    xh, z = lax.axis_index("xh"), lax.axis_index("z")
    place = jnp.stack([lax.axis_index(X), z]).astype(jnp.int32)
    z_only = z.astype(jnp.int32)[None]
    kv_parts = by_head(z_only, key_in, value_in)
    kv_parts, query_in, out_grads = lax.optimization_barrier((kv_parts, query_in, out_grads))
    kv_own = swap_heads(kv_parts)
    kv_oth = tuple(shifted(piece, "xh", 1) for piece in kv_own)
    qg = swap_heads(by_head(z_only, query_in, out_grads))
    where = jnp.stack([xh, z]).astype(jnp.int32)
    attended, near, far = attention(doc_starts, where, kv_own, kv_oth, qg)
    line = ("y", "core", "xh", "z")
    along_y, in_plane = column_moves()
    far = shifted(far, "xh", 1)
    a_near = near_ring(attended, "z")
    a_col = lax.ppermute(attended, line, along_y)
    value_grads = (near + far).astype(jnp.bfloat16)
    g_near = near_ring(value_grads, X)
    g_far = shifted(value_grads, X, 2)
    g_col = lax.ppermute(lax.ppermute(value_grads, line, along_y), line, in_plane)
    a_far = shifted(attended, "z", 2)
    a_col = lax.ppermute(a_col, line, in_plane)
    a_first, a_second = stacked((attended, a_near[0])), stacked((a_near[1], a_far))
    g_first, g_second = stacked((value_grads, g_near[0])), stacked((g_near[1], g_far))
    a_first, a_second, a_col, g_first, g_second, g_col = lax.optimization_barrier(
        (a_first, a_second, a_col, g_first, g_second, g_col)
    )
    cols_a = lax.all_gather(a_col, ("y", "core"), axis=0, tiled=True)
    cols_g = lax.all_gather(g_col, ("y", "core"), axis=0, tiled=True)
    a_firsts, g_firsts = near_ring(a_first, X), near_ring(g_first, "z")
    a_firsts, g_firsts, a_second, g_second = lax.optimization_barrier((a_firsts, g_firsts, a_second, g_second))
    a_seconds, g_seconds = near_ring(a_second, X), near_ring(g_second, "z")
    a_firsts, g_firsts, a_seconds, g_seconds = lax.optimization_barrier((a_firsts, g_firsts, a_seconds, g_seconds))
    a_far = shifted(a_firsts[0], X, 1), shifted(a_seconds[1], X, -1)
    g_far = shifted(g_firsts[0], "z", 1), shifted(g_seconds[1], "z", -1)
    rows_a = halved(((a_first, a_second), *zip(a_firsts, a_seconds), a_far))
    rows_g = halved(((g_first, g_second), *zip(g_firsts, g_seconds), g_far))
    near = ((rows_a, (1, 2), cols_a, along_x_pieces), (rows_g, (0, 1, 2), cols_g, along_z_pieces))
    far = ((rows_a, (0, 3), cols_a, along_x_pieces), (rows_g, (3,), cols_g, along_z_pieces))
    factors = factors_part(place, near, all_tokens, "near_rows")
    return factors_part(place, far, all_tokens, "far_rows", factors)


def solution(mesh):
    split = Mesh(mesh.devices.reshape(4, 2, 2, 4, 2), ("y", "core", "xh", "z", "xl"))
    tokens, features = ("xh", "z"), ("y", "core", "xl")
    spec = P(tokens, features)
    out = P(("y", "core"), ("xh", "z", "xl"))
    return jax.shard_map(
        on_device, mesh=split, in_specs=(spec, spec, spec, spec, P()), out_specs=(out, out),
        check_vma=False,
    )
```

```python
import functools
import math

import jax
import jax.numpy as jnp
from jax import lax
from jax.experimental import pallas as pl
from jax.experimental.pallas import tpu as pltpu
from jax.sharding import Mesh
from jax.sharding import PartitionSpec as P

HEAD_DIM = 128
X = ("xh", "xl")
RING = (0, 3, 1, 2)
MASK_FLOOR = -1e30
KEY_STEP = 512
QUERY_STEP = 512
VMEM_BYTES = 56 * 1024 * 1024


def attention_kernel(starts, where_ref, *refs):
    kv_own, kv_oth, qg = refs[:4], refs[4:8], refs[8:12]
    att_ref, near_ref, far_ref = refs[12:15]
    k_all, v_all, q_ref, g_ref, v_turned, scores, grads, sems = refs[15:]
    half = q_ref.shape[0]
    part = half // 4
    half_id, z = where_ref[0], where_ref[1]
    own_at = pl.multiple_of(half_id * half, half)
    oth_at = pl.multiple_of((1 - half_id) * half, half)
    copies = []
    for pieces, base, targets in (
        (kv_own, own_at, (k_all, v_all)), (kv_oth, oth_at, (k_all, v_all)), (qg, 0, (q_ref, g_ref))
    ):
        for step, piece in zip(RING, pieces):
            at = pl.multiple_of(base + ((z + step) % 4) * part, part)
            for n, target in enumerate(targets):
                copies.append(
                    pltpu.make_async_copy(
                        piece.at[pl.ds(n * part, part)], target.at[pl.ds(at, part)], sems.at[len(copies)]
                    )
                )
    for copy in copies:
        copy.start()
    grads[...] = jnp.zeros_like(grads)
    for copy in copies:
        copy.wait()
    all_tokens = 2 * half
    docs = starts.shape[0]
    for at in range(0, all_tokens, KEY_STEP):
        v_turned[:, at : at + KEY_STEP] = v_all[at : at + KEY_STEP, :].T
    scale = math.log2(math.e) / math.sqrt(HEAD_DIM)
    groups = KEY_STEP // 8

    def query_block(block, carry):
        row = pl.multiple_of(block * QUERY_STEP, QUERY_STEP)
        first = own_at + row
        last = first + QUERY_STEP - 1
        pos = first + lax.broadcasted_iota(jnp.int32, (1, QUERY_STEP), 1)
        begin = jnp.zeros((1, QUERY_STEP), jnp.int32)
        finish = jnp.full((1, QUERY_STEP), all_tokens, jnp.int32)
        lowest, latest = jnp.int32(0), jnp.int32(0)
        highest, soonest = jnp.int32(all_tokens), jnp.int32(all_tokens)
        for d in range(docs):
            start = starts[d]
            lowest = jnp.where(start <= first, jnp.maximum(lowest, start), lowest)
            highest = jnp.where(start > last, jnp.minimum(highest, start), highest)
            latest = jnp.where(start <= last, jnp.maximum(latest, start), latest)
            soonest = jnp.where(start > first, jnp.minimum(soonest, start), soonest)
            begin = jnp.where(start <= pos, jnp.maximum(begin, start), begin)
            finish = jnp.where(start > pos, jnp.minimum(finish, start), finish)
        step_from = lowest // KEY_STEP
        step_to = (highest + KEY_STEP - 1) // KEY_STEP
        inside_from = jnp.minimum((latest + KEY_STEP - 1) // KEY_STEP, step_to)
        inside_to = jnp.maximum(soonest // KEY_STEP, inside_from)
        queries = q_ref[pl.ds(row, QUERY_STEP), :]
        cotangents = g_ref[pl.ds(row, QUERY_STEP), :]
        key_iota = lax.broadcasted_iota(jnp.int32, (KEY_STEP, QUERY_STEP), 0)

        def score_step(step, peak, masked):
            at = pl.multiple_of(step * KEY_STEP, KEY_STEP)
            s = lax.dot_general(
                k_all[pl.ds(at, KEY_STEP), :], queries, (((1,), (1,)), ((), ())),
                preferred_element_type=jnp.float32,
            ) * scale
            if masked:
                allowed = (key_iota >= begin - at) & (key_iota < finish - at)
                s = jnp.where(allowed, s, MASK_FLOOR)
            scores[pl.ds(at, KEY_STEP), :] = s
            return jnp.maximum(peak, jnp.max(s.reshape(groups, 8, QUERY_STEP), axis=0))

        edge_step = functools.partial(score_step, masked=True)
        inside_step = functools.partial(score_step, masked=False)
        peak = jnp.full((8, QUERY_STEP), MASK_FLOOR, jnp.float32)
        peak = lax.fori_loop(step_from, inside_from, edge_step, peak)
        peak = lax.fori_loop(inside_from, inside_to, inside_step, peak)
        peak = lax.fori_loop(inside_to, step_to, edge_step, peak)
        peak = jnp.max(peak, axis=0, keepdims=True)

        def mass_step(step, mass):
            at = pl.multiple_of(step * KEY_STEP, KEY_STEP)
            e = jnp.exp2(scores[pl.ds(at, KEY_STEP), :] - peak)
            scores[pl.ds(at, KEY_STEP), :] = e
            return mass + jnp.sum(e.reshape(groups, 8, QUERY_STEP), axis=0)

        mass = lax.fori_loop(step_from, step_to, mass_step, jnp.zeros((8, QUERY_STEP), jnp.float32))
        share = 1.0 / jnp.sum(mass, axis=0, keepdims=True)

        def value_step(step, summed):
            at = pl.multiple_of(step * KEY_STEP, KEY_STEP)
            w = (scores[pl.ds(at, KEY_STEP), :] * share).astype(jnp.bfloat16)
            grads[pl.ds(at, KEY_STEP), :] += jnp.dot(
                w, cotangents, preferred_element_type=jnp.float32
            )
            return summed + jnp.dot(
                v_turned[:, pl.ds(at, KEY_STEP)], w, preferred_element_type=jnp.float32
            )

        summed = lax.fori_loop(
            step_from, step_to, value_step, jnp.zeros((HEAD_DIM, QUERY_STEP), jnp.float32)
        )
        att_ref[:, pl.ds(row, QUERY_STEP)] = summed.astype(jnp.bfloat16)
        return carry

    lax.fori_loop(0, half // QUERY_STEP, query_block, 0)
    for at in range(0, half, KEY_STEP):
        near_ref[:, at : at + KEY_STEP] = grads[pl.ds(own_at + at, KEY_STEP), :].T
        far_ref[:, at : at + KEY_STEP] = grads[pl.ds(oth_at + at, KEY_STEP), :].T.astype(jnp.bfloat16)


def attention(starts, where, kv_own, kv_oth, qg):
    half = 2 * qg[0].shape[0]
    hbm = pl.BlockSpec(memory_space=pl.ANY)
    vmem = pl.BlockSpec(memory_space=pltpu.VMEM)
    smem = pl.BlockSpec(memory_space=pltpu.SMEM)
    return pl.pallas_call(
        attention_kernel,
        out_shape=(
            jax.ShapeDtypeStruct((HEAD_DIM, half), jnp.bfloat16),
            jax.ShapeDtypeStruct((HEAD_DIM, half), jnp.float32),
            jax.ShapeDtypeStruct((HEAD_DIM, half), jnp.bfloat16),
        ),
        in_specs=[smem, smem] + [hbm] * 12,
        out_specs=(vmem, vmem, vmem),
        scratch_shapes=[
            pltpu.VMEM((2 * half, HEAD_DIM), jnp.bfloat16),
            pltpu.VMEM((2 * half, HEAD_DIM), jnp.bfloat16),
            pltpu.VMEM((half, HEAD_DIM), jnp.bfloat16),
            pltpu.VMEM((half, HEAD_DIM), jnp.bfloat16),
            pltpu.VMEM((HEAD_DIM, 2 * half), jnp.bfloat16),
            pltpu.VMEM((2 * half, QUERY_STEP), jnp.float32),
            pltpu.VMEM((2 * half, HEAD_DIM), jnp.float32),
            pltpu.SemaphoreType.DMA((24,)),
        ],
        compiler_params=pltpu.CompilerParams(vmem_limit_bytes=VMEM_BYTES),
        name="attention",
    )(starts, where, *kv_own, *kv_oth, *qg)


def shifted(x, axis, by):
    count = lax.axis_size(axis)
    return lax.ppermute(x, axis, [(i, (i + by) % count) for i in range(count)])


def near_ring(x, axis):
    return shifted(x, axis, 1), shifted(x, axis, -1)


def heads_kernel(z_ref, *refs):
    sources, outs, sems = refs[:2], refs[2:6], refs[6]
    rows = sources[0].shape[0]
    copies = []
    for k, out in enumerate(outs):
        head = (z_ref[0] + k) % 4
        for n, source in enumerate(sources):
            copies.append(
                pltpu.make_async_copy(
                    source.at[:, pl.ds(pl.multiple_of(head * HEAD_DIM, HEAD_DIM), HEAD_DIM)],
                    out.at[pl.ds(n * rows, rows)], sems.at[len(copies)],
                )
            )
    for copy in copies:
        copy.start()
    for copy in copies:
        copy.wait()


def by_head(z, first, second):
    rows = first.shape[0]
    shape = jax.ShapeDtypeStruct((2 * rows, HEAD_DIM), first.dtype)
    hbm = pl.BlockSpec(memory_space=pl.ANY)
    vmem = pl.BlockSpec(memory_space=pltpu.VMEM)
    return pl.pallas_call(
        heads_kernel,
        out_shape=(shape,) * 4,
        in_specs=[pl.BlockSpec(memory_space=pltpu.SMEM), hbm, hbm],
        out_specs=(vmem,) * 4,
        scratch_shapes=[pltpu.SemaphoreType.DMA((8,))],
        name="by_head",
    )(z, first, second)


def swap_heads(parts):
    return parts[0], shifted(parts[1], "z", 1), shifted(parts[3], "z", -1), shifted(parts[2], "z", 2)


def stack_kernel(*refs):
    out, at = refs[-1], 0
    for part in refs[:-1]:
        out[at : at + part.shape[0], :] = part[...]
        at += part.shape[0]


def stacked(parts):
    rows = sum(p.shape[0] for p in parts)
    vmem = pl.BlockSpec(memory_space=pltpu.VMEM)
    return pl.pallas_call(
        stack_kernel,
        out_shape=jax.ShapeDtypeStruct((rows, *parts[0].shape[1:]), parts[0].dtype),
        in_specs=[vmem] * len(parts),
        out_specs=vmem,
        name="stack",
    )(*parts)


def factors_kernel(place, *refs, count, jobs, aliased):
    n_in = sum(job[0] + 1 for job in jobs)
    refs = list(refs)
    inputs, refs = refs[:n_in], refs[n_in + 2 * aliased :]
    outs, scratch = refs[: len(jobs)], refs[len(jobs) :]
    x, z = place[0], place[1]
    block = HEAD_DIM
    line = 8 - (x // 2) * 2 - z // 2 - 2 * (z % 2)
    waits, out_rows = [], []
    for j, (n_pieces, plan, _) in enumerate(jobs):
        rows, cols, sems = scratch[4 * j], scratch[4 * j + 1], scratch[4 * j + 3]
        pieces, col_ref = inputs[:n_pieces], inputs[n_pieces]
        inputs = inputs[n_pieces + 1 :]
        copies = []
        for n in range(8):
            at = pl.multiple_of(((n // 2 + line) % 4) * block, block)
            copies.append((col_ref.at[pl.ds(n * block, block)], cols.at[n % 2, pl.ds(at, block)]))
        targets, to = plan(x, z)
        for piece, pair in zip(pieces, targets):
            for n, (which, local) in enumerate(pair):
                at = pl.multiple_of(local * block, block)
                copies.append((piece.at[pl.ds(n * block, block)], rows.at[which, pl.ds(at, block)]))
        waits.append([pltpu.make_async_copy(src, dst, sems.at[k]) for k, (src, dst) in enumerate(copies)])
        out_rows.append(to)
        for copy in waits[-1]:
            copy.start()
    stores = []
    for j, (_, _, blocks) in enumerate(jobs):
        rows, cols, result, sems = scratch[4 * j : 4 * j + 4]
        for copy in waits[j]:
            copy.wait()
        total = None
        for which in range(2):
            part = lax.dot_general(
                rows[which], cols[which], (((1,), (1,)), ((), ())), preferred_element_type=jnp.float32
            )
            total = part if total is None else total + part
        result[...] = total * (1.0 / count)
        for local in range(blocks):
            row = pl.multiple_of(out_rows[j][local] * block, block)
            store = pltpu.make_async_copy(
                result.at[pl.ds(local * block, block)], outs[j].at[pl.ds(row, block)], sems.at[24 + local]
            )
            store.start()
            stores.append(store)
    for store in stores:
        store.wait()


def along_x_pieces(pieces):
    def plan(x, z):
        targets = [[((x + RING[outer]) % 4 // 2, slot) for slot in slots] for outer, slots in pieces]
        cols_at = (x + RING[pieces[0][0]]) % 2
        return targets, [cols_at * 4 + (z + RING[slot]) % 4 for slot in range(4)]

    return plan, 4


def along_z_pieces(pieces):
    groups = list(dict.fromkeys(outer for outer, _ in pieces))

    def plan(x, z):
        targets = []
        for outer, slots in pieces:
            at = [(x + RING[slot]) % 4 for slot in slots]
            targets.append([(xx // 2, groups.index(outer) * 2 + xx % 2) for xx in at])
        return targets, [c * 4 + (z + RING[g]) % 4 for g in groups for c in range(2)]

    return plan, 2 * len(groups)


def halved(groups):
    return [(outer, slots, groups[outer][n]) for outer in range(4) for n, slots in enumerate(((0, 1), (2, 3)))]


def factors_part(place, jobs, count, name, into=()):
    args, plans, scratch = [place], [], []
    for pieces, outers, cols, layout in jobs:
        held = [piece for piece in pieces if piece[0] in outers]
        plan, blocks = layout([(outer, slots) for outer, slots, _ in held])
        args += [array for _, _, array in held] + [cols]
        plans.append((len(held), plan, blocks))
        scratch += [
            pltpu.VMEM((2, blocks * HEAD_DIM, cols.shape[1]), jnp.bfloat16),
            pltpu.VMEM((2, 4 * HEAD_DIM, cols.shape[1]), jnp.bfloat16),
            pltpu.VMEM((blocks * HEAD_DIM, 4 * HEAD_DIM), jnp.float32),
            pltpu.SemaphoreType.DMA((32,)),
        ]
    hbm = pl.BlockSpec(memory_space=pl.ANY)
    aliased = len(into) > 0
    kernel = functools.partial(factors_kernel, count=count, jobs=plans, aliased=int(aliased))
    shape = jax.ShapeDtypeStruct((8 * HEAD_DIM, 4 * HEAD_DIM), jnp.float32)
    return pl.pallas_call(
        kernel,
        out_shape=(shape, shape),
        in_specs=[pl.BlockSpec(memory_space=pltpu.SMEM)] + [hbm] * (len(args) + len(into) - 1),
        out_specs=(hbm, hbm),
        input_output_aliases={len(args): 0, len(args) + 1: 1} if aliased else {},
        scratch_shapes=scratch,
        compiler_params=pltpu.CompilerParams(vmem_limit_bytes=VMEM_BYTES),
        name=name,
    )(*args, *into)


def column_moves():
    ranks = [(y, core, xh, z) for y in range(4) for core in range(2) for xh in range(2) for z in range(4)]
    place = {rank: n for n, rank in enumerate(ranks)}
    along_y, in_plane = [], []
    for y, core, xh, z in ranks:
        spread = (y + z + 2 * core) % 4
        along_y.append((place[y, core, xh, z], place[spread, core, xh, z]))
        in_plane.append((place[spread, core, xh, z], place[spread, xh, y // 2, (y % 2) * 2 + core]))
    return along_y, in_plane


def on_device(query_in, key_in, value_in, out_grads, doc_starts):
    all_tokens = query_in.shape[0] * 8
    xh, z = lax.axis_index("xh"), lax.axis_index("z")
    place = jnp.stack([lax.axis_index(X), z]).astype(jnp.int32)
    z_only = z.astype(jnp.int32)[None]
    kv_parts = by_head(z_only, key_in, value_in)
    own, below, above, across = swap_heads(kv_parts)
    below, above, query_in, out_grads = lax.optimization_barrier((below, above, query_in, out_grads))
    kv_own = (own, below, above, across)
    kv_oth = tuple(shifted(piece, "xh", 1) for piece in kv_own)
    qg = swap_heads(by_head(z_only, query_in, out_grads))
    where = jnp.stack([xh, z]).astype(jnp.int32)
    attended, near, far = attention(doc_starts, where, kv_own, kv_oth, qg)
    line = ("y", "core", "xh", "z")
    along_y, in_plane = column_moves()
    far = shifted(far, "xh", 1)
    a_near = near_ring(attended, "z")
    a_col = lax.ppermute(attended, line, along_y)
    value_grads = (near + far).astype(jnp.bfloat16)
    g_near = near_ring(value_grads, X)
    g_far = shifted(value_grads, X, 2)
    g_col = lax.ppermute(lax.ppermute(value_grads, line, along_y), line, in_plane)
    a_far = shifted(attended, "z", 2)
    a_col = lax.ppermute(a_col, line, in_plane)
    a_first, a_second = stacked((attended, a_near[0])), stacked((a_near[1], a_far))
    g_first, g_second = stacked((value_grads, g_near[0])), stacked((g_near[1], g_far))
    a_first, a_second, a_col, g_first, g_second, g_col = lax.optimization_barrier(
        (a_first, a_second, a_col, g_first, g_second, g_col)
    )
    cols_a = lax.all_gather(a_col, ("y", "core"), axis=0, tiled=True)
    cols_g = lax.all_gather(g_col, ("y", "core"), axis=0, tiled=True)
    a_firsts, g_firsts = near_ring(a_first, X), near_ring(g_first, "z")
    a_firsts, g_firsts, a_second, g_second = lax.optimization_barrier((a_firsts, g_firsts, a_second, g_second))
    a_seconds, g_seconds = near_ring(a_second, X), near_ring(g_second, "z")
    a_firsts, g_firsts, a_seconds, g_seconds = lax.optimization_barrier((a_firsts, g_firsts, a_seconds, g_seconds))
    a_far = shifted(a_firsts[0], X, 1), shifted(a_seconds[1], X, -1)
    g_far = shifted(g_firsts[0], "z", 1), shifted(g_seconds[1], "z", -1)
    rows_a = halved(((a_first, a_second), *zip(a_firsts, a_seconds), a_far))
    rows_g = halved(((g_first, g_second), *zip(g_firsts, g_seconds), g_far))
    near = ((rows_a, (1, 2), cols_a, along_x_pieces), (rows_g, (0, 1, 2), cols_g, along_z_pieces))
    far = ((rows_a, (0, 3), cols_a, along_x_pieces), (rows_g, (3,), cols_g, along_z_pieces))
    factors = factors_part(place, near, all_tokens, "near_rows")
    return factors_part(place, far, all_tokens, "far_rows", factors)


def solution(mesh):
    split = Mesh(mesh.devices.reshape(4, 2, 2, 4, 2), ("y", "core", "xh", "z", "xl"))
    tokens, features = ("xh", "z"), ("y", "core", "xl")
    spec = P(tokens, features)
    out = P(("y", "core"), ("xh", "z", "xl"))
    return jax.shard_map(
        on_device, mesh=split, in_specs=(spec, spec, spec, spec, P()), out_specs=(out, out),
        check_vma=False,
    )
```

```python
import functools
import math

import jax
import jax.numpy as jnp
from jax import lax
from jax.experimental import pallas as pl
from jax.experimental.pallas import tpu as pltpu
from jax.sharding import Mesh
from jax.sharding import PartitionSpec as P

HEAD_DIM = 128
X = ("xh", "xl")
RING = (0, 3, 1, 2)
MASK_FLOOR = -1e30
KEY_STEP = 512
QUERY_STEP = 512
VMEM_BYTES = 56 * 1024 * 1024


def attention_kernel(starts, where_ref, *refs):
    kv_own, kv_oth, qg = refs[:4], refs[4:8], refs[8:12]
    att_ref, near_ref, far_ref = refs[12:15]
    k_all, v_all, q_ref, g_ref, v_turned, scores, grads, sems = refs[15:]
    half = q_ref.shape[0]
    part = half // 4
    half_id, z = where_ref[0], where_ref[1]
    own_at = pl.multiple_of(half_id * half, half)
    oth_at = pl.multiple_of((1 - half_id) * half, half)
    copies = []
    for pieces, base, targets in (
        (kv_own, own_at, (k_all, v_all)), (kv_oth, oth_at, (k_all, v_all)), (qg, 0, (q_ref, g_ref))
    ):
        for step, piece in zip(RING, pieces):
            at = pl.multiple_of(base + ((z + step) % 4) * part, part)
            for n, target in enumerate(targets):
                copies.append(
                    pltpu.make_async_copy(
                        piece.at[pl.ds(n * part, part)], target.at[pl.ds(at, part)], sems.at[len(copies)]
                    )
                )
    for copy in copies:
        copy.start()
    grads[...] = jnp.zeros_like(grads)
    for copy in copies:
        copy.wait()
    all_tokens = 2 * half
    docs = starts.shape[0]
    for at in range(0, all_tokens, KEY_STEP):
        v_turned[:, at : at + KEY_STEP] = v_all[at : at + KEY_STEP, :].T
    scale = math.log2(math.e) / math.sqrt(HEAD_DIM)
    groups = KEY_STEP // 8

    def query_block(block, carry):
        row = pl.multiple_of(block * QUERY_STEP, QUERY_STEP)
        first = own_at + row
        last = first + QUERY_STEP - 1
        pos = first + lax.broadcasted_iota(jnp.int32, (1, QUERY_STEP), 1)
        begin = jnp.zeros((1, QUERY_STEP), jnp.int32)
        finish = jnp.full((1, QUERY_STEP), all_tokens, jnp.int32)
        lowest, latest = jnp.int32(0), jnp.int32(0)
        highest, soonest = jnp.int32(all_tokens), jnp.int32(all_tokens)
        for d in range(docs):
            start = starts[d]
            lowest = jnp.where(start <= first, jnp.maximum(lowest, start), lowest)
            highest = jnp.where(start > last, jnp.minimum(highest, start), highest)
            latest = jnp.where(start <= last, jnp.maximum(latest, start), latest)
            soonest = jnp.where(start > first, jnp.minimum(soonest, start), soonest)
            begin = jnp.where(start <= pos, jnp.maximum(begin, start), begin)
            finish = jnp.where(start > pos, jnp.minimum(finish, start), finish)
        step_from = lowest // KEY_STEP
        step_to = (highest + KEY_STEP - 1) // KEY_STEP
        inside_from = jnp.minimum((latest + KEY_STEP - 1) // KEY_STEP, step_to)
        inside_to = jnp.maximum(soonest // KEY_STEP, inside_from)
        queries = q_ref[pl.ds(row, QUERY_STEP), :]
        cotangents = g_ref[pl.ds(row, QUERY_STEP), :]
        key_iota = lax.broadcasted_iota(jnp.int32, (KEY_STEP, QUERY_STEP), 0)

        def score_step(step, peak, masked):
            at = pl.multiple_of(step * KEY_STEP, KEY_STEP)
            s = lax.dot_general(
                k_all[pl.ds(at, KEY_STEP), :], queries, (((1,), (1,)), ((), ())),
                preferred_element_type=jnp.float32,
            ) * scale
            if masked:
                allowed = (key_iota >= begin - at) & (key_iota < finish - at)
                s = jnp.where(allowed, s, MASK_FLOOR)
            scores[pl.ds(at, KEY_STEP), :] = s
            return jnp.maximum(peak, jnp.max(s.reshape(groups, 8, QUERY_STEP), axis=0))

        edge_step = functools.partial(score_step, masked=True)
        inside_step = functools.partial(score_step, masked=False)
        peak = jnp.full((8, QUERY_STEP), MASK_FLOOR, jnp.float32)
        peak = lax.fori_loop(step_from, inside_from, edge_step, peak)
        peak = lax.fori_loop(inside_from, inside_to, inside_step, peak)
        peak = lax.fori_loop(inside_to, step_to, edge_step, peak)
        peak = jnp.max(peak, axis=0, keepdims=True)

        def mass_step(step, mass):
            at = pl.multiple_of(step * KEY_STEP, KEY_STEP)
            e = jnp.exp2(scores[pl.ds(at, KEY_STEP), :] - peak)
            scores[pl.ds(at, KEY_STEP), :] = e
            return mass + jnp.sum(e.reshape(groups, 8, QUERY_STEP), axis=0)

        mass = lax.fori_loop(step_from, step_to, mass_step, jnp.zeros((8, QUERY_STEP), jnp.float32))
        share = 1.0 / jnp.sum(mass, axis=0, keepdims=True)

        def value_step(step, summed):
            at = pl.multiple_of(step * KEY_STEP, KEY_STEP)
            w = (scores[pl.ds(at, KEY_STEP), :] * share).astype(jnp.bfloat16)
            grads[pl.ds(at, KEY_STEP), :] += jnp.dot(
                w, cotangents, preferred_element_type=jnp.float32
            )
            return summed + jnp.dot(
                v_turned[:, pl.ds(at, KEY_STEP)], w, preferred_element_type=jnp.float32
            )

        summed = lax.fori_loop(
            step_from, step_to, value_step, jnp.zeros((HEAD_DIM, QUERY_STEP), jnp.float32)
        )
        att_ref[:, pl.ds(row, QUERY_STEP)] = summed.astype(jnp.bfloat16)
        return carry

    lax.fori_loop(0, half // QUERY_STEP, query_block, 0)
    for at in range(0, half, KEY_STEP):
        near_ref[:, at : at + KEY_STEP] = grads[pl.ds(own_at + at, KEY_STEP), :].T
        far_ref[:, at : at + KEY_STEP] = grads[pl.ds(oth_at + at, KEY_STEP), :].T.astype(jnp.bfloat16)


def attention(starts, where, kv_own, kv_oth, qg):
    half = 2 * qg[0].shape[0]
    hbm = pl.BlockSpec(memory_space=pl.ANY)
    vmem = pl.BlockSpec(memory_space=pltpu.VMEM)
    smem = pl.BlockSpec(memory_space=pltpu.SMEM)
    return pl.pallas_call(
        attention_kernel,
        out_shape=(
            jax.ShapeDtypeStruct((HEAD_DIM, half), jnp.bfloat16),
            jax.ShapeDtypeStruct((HEAD_DIM, half), jnp.float32),
            jax.ShapeDtypeStruct((HEAD_DIM, half), jnp.bfloat16),
        ),
        in_specs=[smem, smem] + [hbm] * 12,
        out_specs=(vmem, vmem, vmem),
        scratch_shapes=[
            pltpu.VMEM((2 * half, HEAD_DIM), jnp.bfloat16),
            pltpu.VMEM((2 * half, HEAD_DIM), jnp.bfloat16),
            pltpu.VMEM((half, HEAD_DIM), jnp.bfloat16),
            pltpu.VMEM((half, HEAD_DIM), jnp.bfloat16),
            pltpu.VMEM((HEAD_DIM, 2 * half), jnp.bfloat16),
            pltpu.VMEM((2 * half, QUERY_STEP), jnp.float32),
            pltpu.VMEM((2 * half, HEAD_DIM), jnp.float32),
            pltpu.SemaphoreType.DMA((24,)),
        ],
        compiler_params=pltpu.CompilerParams(vmem_limit_bytes=VMEM_BYTES),
        name="attention",
    )(starts, where, *kv_own, *kv_oth, *qg)


def shifted(x, axis, by):
    count = lax.axis_size(axis)
    return lax.ppermute(x, axis, [(i, (i + by) % count) for i in range(count)])


def near_ring(x, axis):
    return shifted(x, axis, 1), shifted(x, axis, -1)


def heads_kernel(z_ref, *refs):
    sources, outs, sems = refs[:2], refs[2:6], refs[6]
    rows = sources[0].shape[0]
    copies = []
    for k, out in enumerate(outs):
        head = (z_ref[0] + k) % 4
        for n, source in enumerate(sources):
            copies.append(
                pltpu.make_async_copy(
                    source.at[:, pl.ds(pl.multiple_of(head * HEAD_DIM, HEAD_DIM), HEAD_DIM)],
                    out.at[pl.ds(n * rows, rows)], sems.at[len(copies)],
                )
            )
    for copy in copies:
        copy.start()
    for copy in copies:
        copy.wait()


def by_head(z, first, second):
    rows = first.shape[0]
    shape = jax.ShapeDtypeStruct((2 * rows, HEAD_DIM), first.dtype)
    hbm = pl.BlockSpec(memory_space=pl.ANY)
    vmem = pl.BlockSpec(memory_space=pltpu.VMEM)
    return pl.pallas_call(
        heads_kernel,
        out_shape=(shape,) * 4,
        in_specs=[pl.BlockSpec(memory_space=pltpu.SMEM), hbm, hbm],
        out_specs=(vmem,) * 4,
        scratch_shapes=[pltpu.SemaphoreType.DMA((8,))],
        name="by_head",
    )(z, first, second)


def swap_heads(parts):
    return parts[0], shifted(parts[1], "z", 1), shifted(parts[3], "z", -1), shifted(parts[2], "z", 2)


def stack_kernel(*refs):
    out, at = refs[-1], 0
    for part in refs[:-1]:
        out[at : at + part.shape[0], :] = part[...]
        at += part.shape[0]


def stacked(parts):
    rows = sum(p.shape[0] for p in parts)
    vmem = pl.BlockSpec(memory_space=pltpu.VMEM)
    return pl.pallas_call(
        stack_kernel,
        out_shape=jax.ShapeDtypeStruct((rows, *parts[0].shape[1:]), parts[0].dtype),
        in_specs=[vmem] * len(parts),
        out_specs=vmem,
        name="stack",
    )(*parts)


def factors_kernel(place, *refs, count, jobs, aliased):
    n_in = sum(job[0] + 1 for job in jobs)
    refs = list(refs)
    inputs, refs = refs[:n_in], refs[n_in + 2 * aliased :]
    outs, scratch = refs[: len(jobs)], refs[len(jobs) :]
    x, z = place[0], place[1]
    block = HEAD_DIM
    line = 8 - (x // 2) * 2 - z // 2 - 2 * (z % 2)
    waits, out_rows = [], []
    for j, (n_pieces, plan, _) in enumerate(jobs):
        rows, cols, sems = scratch[4 * j], scratch[4 * j + 1], scratch[4 * j + 3]
        pieces, col_ref = inputs[:n_pieces], inputs[n_pieces]
        inputs = inputs[n_pieces + 1 :]
        copies = []
        for n in range(8):
            at = pl.multiple_of(((n // 2 + line) % 4) * block, block)
            copies.append((col_ref.at[pl.ds(n * block, block)], cols.at[n % 2, pl.ds(at, block)]))
        targets, to = plan(x, z)
        for piece, pair in zip(pieces, targets):
            for n, (which, local) in enumerate(pair):
                at = pl.multiple_of(local * block, block)
                copies.append((piece.at[pl.ds(n * block, block)], rows.at[which, pl.ds(at, block)]))
        waits.append([pltpu.make_async_copy(src, dst, sems.at[k]) for k, (src, dst) in enumerate(copies)])
        out_rows.append(to)
        for copy in waits[-1]:
            copy.start()
    stores = []
    for j, (_, _, blocks) in enumerate(jobs):
        rows, cols, result, sems = scratch[4 * j : 4 * j + 4]
        for copy in waits[j]:
            copy.wait()
        total = None
        for which in range(2):
            part = lax.dot_general(
                rows[which], cols[which], (((1,), (1,)), ((), ())), preferred_element_type=jnp.float32
            )
            total = part if total is None else total + part
        result[...] = total * (1.0 / count)
        for local in range(blocks):
            row = pl.multiple_of(out_rows[j][local] * block, block)
            store = pltpu.make_async_copy(
                result.at[pl.ds(local * block, block)], outs[j].at[pl.ds(row, block)], sems.at[24 + local]
            )
            store.start()
            stores.append(store)
    for store in stores:
        store.wait()


def along_x_pieces(pieces):
    def plan(x, z):
        targets = [[((x + RING[outer]) % 4 // 2, slot) for slot in slots] for outer, slots in pieces]
        cols_at = (x + RING[pieces[0][0]]) % 2
        return targets, [cols_at * 4 + (z + RING[slot]) % 4 for slot in range(4)]

    return plan, 4


def along_z_pieces(pieces):
    groups = list(dict.fromkeys(outer for outer, _ in pieces))

    def plan(x, z):
        targets = []
        for outer, slots in pieces:
            at = [(x + RING[slot]) % 4 for slot in slots]
            targets.append([(xx // 2, groups.index(outer) * 2 + xx % 2) for xx in at])
        return targets, [c * 4 + (z + RING[g]) % 4 for g in groups for c in range(2)]

    return plan, 2 * len(groups)


def halved(groups):
    return [(outer, slots, groups[outer][n]) for outer in range(4) for n, slots in enumerate(((0, 1), (2, 3)))]


def factors_part(place, jobs, count, name, into=()):
    args, plans, scratch = [place], [], []
    for pieces, outers, cols, layout in jobs:
        held = [piece for piece in pieces if piece[0] in outers]
        plan, blocks = layout([(outer, slots) for outer, slots, _ in held])
        args += [array for _, _, array in held] + [cols]
        plans.append((len(held), plan, blocks))
        scratch += [
            pltpu.VMEM((2, blocks * HEAD_DIM, cols.shape[1]), jnp.bfloat16),
            pltpu.VMEM((2, 4 * HEAD_DIM, cols.shape[1]), jnp.bfloat16),
            pltpu.VMEM((blocks * HEAD_DIM, 4 * HEAD_DIM), jnp.float32),
            pltpu.SemaphoreType.DMA((32,)),
        ]
    hbm = pl.BlockSpec(memory_space=pl.ANY)
    aliased = len(into) > 0
    kernel = functools.partial(factors_kernel, count=count, jobs=plans, aliased=int(aliased))
    shape = jax.ShapeDtypeStruct((8 * HEAD_DIM, 4 * HEAD_DIM), jnp.float32)
    return pl.pallas_call(
        kernel,
        out_shape=(shape, shape),
        in_specs=[pl.BlockSpec(memory_space=pltpu.SMEM)] + [hbm] * (len(args) + len(into) - 1),
        out_specs=(hbm, hbm),
        input_output_aliases={len(args): 0, len(args) + 1: 1} if aliased else {},
        scratch_shapes=scratch,
        compiler_params=pltpu.CompilerParams(vmem_limit_bytes=VMEM_BYTES),
        name=name,
    )(*args, *into)


def column_moves():
    ranks = [(y, core, xh, z) for y in range(4) for core in range(2) for xh in range(2) for z in range(4)]
    place = {rank: n for n, rank in enumerate(ranks)}
    along_y, in_plane = [], []
    for y, core, xh, z in ranks:
        spread = (y + z + 2 * core) % 4
        along_y.append((place[y, core, xh, z], place[spread, core, xh, z]))
        in_plane.append((place[spread, core, xh, z], place[spread, xh, y // 2, (y % 2) * 2 + core]))
    return along_y, in_plane


def on_device(query_in, key_in, value_in, out_grads, doc_starts):
    all_tokens = query_in.shape[0] * 8
    xh, z = lax.axis_index("xh"), lax.axis_index("z")
    place = jnp.stack([lax.axis_index(X), z]).astype(jnp.int32)
    z_only = z.astype(jnp.int32)[None]
    kv_parts = by_head(z_only, key_in, value_in)
    own, below, above, across = swap_heads(kv_parts)
    below, above, query_in, out_grads = lax.optimization_barrier((below, above, query_in, out_grads))
    kv_own = (own, below, above, across)
    kv_oth = tuple(shifted(piece, "xh", 1) for piece in kv_own)
    qg = swap_heads(by_head(z_only, query_in, out_grads))
    where = jnp.stack([xh, z]).astype(jnp.int32)
    attended, near, far = attention(doc_starts, where, kv_own, kv_oth, qg)
    line = ("y", "core", "xh", "z")
    along_y, in_plane = column_moves()
    far = shifted(far, "xh", 1)
    a_near = near_ring(attended, "z")
    a_col = lax.ppermute(attended, line, along_y)
    value_grads = (near + far).astype(jnp.bfloat16)
    g_near = near_ring(value_grads, X)
    g_far = shifted(value_grads, X, 2)
    g_col = lax.ppermute(lax.ppermute(value_grads, line, along_y), line, in_plane)
    tile, far = lax.optimization_barrier((attended, far))
    a_far = shifted(tile, "z", 2)
    a_col = lax.ppermute(a_col, line, in_plane)
    a_first, a_second = stacked((attended, a_near[0])), stacked((a_near[1], a_far))
    g_first, g_second = stacked((value_grads, g_near[0])), stacked((g_near[1], g_far))
    a_first, a_second, a_col, g_first, g_second, g_col = lax.optimization_barrier(
        (a_first, a_second, a_col, g_first, g_second, g_col)
    )
    cols_a = lax.all_gather(a_col, ("y", "core"), axis=0, tiled=True)
    cols_g = lax.all_gather(g_col, ("y", "core"), axis=0, tiled=True)
    a_firsts, g_firsts = near_ring(a_first, X), near_ring(g_first, "z")
    a_firsts, g_firsts, a_second, g_second = lax.optimization_barrier((a_firsts, g_firsts, a_second, g_second))
    a_seconds, g_seconds = near_ring(a_second, X), near_ring(g_second, "z")
    a_firsts, g_firsts, a_seconds, g_seconds = lax.optimization_barrier((a_firsts, g_firsts, a_seconds, g_seconds))
    a_far = shifted(a_firsts[0], X, 1), shifted(a_seconds[1], X, -1)
    g_far = shifted(g_firsts[0], "z", 1), shifted(g_seconds[1], "z", -1)
    rows_a = halved(((a_first, a_second), *zip(a_firsts, a_seconds), a_far))
    rows_g = halved(((g_first, g_second), *zip(g_firsts, g_seconds), g_far))
    near = ((rows_a, (1, 2), cols_a, along_x_pieces), (rows_g, (0, 1, 2), cols_g, along_z_pieces))
    far = ((rows_a, (0, 3), cols_a, along_x_pieces), (rows_g, (3,), cols_g, along_z_pieces))
    factors = factors_part(place, near, all_tokens, "near_rows")
    return factors_part(place, far, all_tokens, "far_rows", factors)


def solution(mesh):
    split = Mesh(mesh.devices.reshape(4, 2, 2, 4, 2), ("y", "core", "xh", "z", "xl"))
    tokens, features = ("xh", "z"), ("y", "core", "xl")
    spec = P(tokens, features)
    out = P(("y", "core"), ("xh", "z", "xl"))
    return jax.shard_map(
        on_device, mesh=split, in_specs=(spec, spec, spec, spec, P()), out_specs=(out, out),
        check_vma=False,
    )
```
